32 devices in a mesh: blk: 8 (over y, x, core), rows: 4 (over z).
Axes of the slice: x: 2, y: 2, z: 4, core: 2. Of those that a mesh axis runs over, the one named last changes fastest.
Arguments:
- sens_tiles: bfloat16 [2048, 512, 128], P('blk', 'rows'), may hold values from -1 to 1
- start_basis: bfloat16 [64, 32768], P(None, 'blk'), may hold values from -6 to 6
- row_blocks: int32 [2048, 4], P('blk', 'rows'), may hold values from 0 to 7, as said below
- col_blocks: int32 [2048, 4], P('blk', 'rows'), may hold values from 0 to 31, as said below
- live_counts: int32 [8, 4], P('blk', 'rows'), may hold values from 64 to 256, as said below
Outputs:
- orthonormal: float32 [4, 64, 32768], P(None, None, ('blk', 'rows'))
The draws below stay inside these ranges and needn't reach their ends.
Inputs may be any that keep to these rules, and one draw needn't show every extreme that they name: Within one device the pairs (row_blocks, col_blocks) of its 256 slots are distinct. Within one device the pairs (row_blocks, col_blocks) of its 256 slots are distinct. Slots 0 to live_counts - 1 of a device hold its tiles; some device has all 256 slots live.
All inputs are finite; a program needn't handle non-finite values.
Results may differ from the reference program's by a relative error of at most 0.012.
The reference program's roundings to bfloat16 on the way count: a program that leaves them out, or rounds other values in their place, can miss the bound.
Values may be sent and summed in bfloat16 or wider, within the bound.
A program may use at most 128 MiB of HBM per device.

```python
import math
import jax
import jax.numpy as jnp
from jax import lax

TILE = 128
K = 64
RB = 8
CB = 32
MAXB = 256
ITERS = 4
DATA = 4096
CELLS = 32768
SLOTS = 2048
N_BLK = 8
N_ROWS = 4


grade_span = 3.28


def pattern_pairs(key):
    base = jax.random.fold_in(key, 7)
    keys = jax.random.split(base, N_BLK * N_ROWS)
    orders = jax.vmap(lambda single: jax.random.permutation(single, RB * CB))(keys)[:, :MAXB]
    rows_part = (orders // CB).reshape(N_BLK, N_ROWS, MAXB).transpose(0, 2, 1).reshape(N_BLK * MAXB, N_ROWS)
    cols_part = (orders % CB).reshape(N_BLK, N_ROWS, MAXB).transpose(0, 2, 1).reshape(N_BLK * MAXB, N_ROWS)
    return (rows_part.astype(jnp.int32), cols_part.astype(jnp.int32))


def draw_sens_tiles(key, part):
    rows_part = pattern_pairs(key)[0]
    datum_block = jnp.arange(N_ROWS, dtype=jnp.int32)[None, :] * RB + rows_part
    datum_index = datum_block[:, :, None] * TILE + jnp.arange(TILE, dtype=jnp.int32)[None, None, :]
    ranking = jax.random.permutation(jax.random.fold_in(key, 13), DATA)
    levels = jnp.minimum(ranking, K).astype(jnp.float32) / K
    weights = jnp.exp(-grade_span * levels)
    row_scale = jnp.take(weights, datum_index.reshape(-1)).reshape(SLOTS, N_ROWS * TILE)
    noise_key = jax.random.fold_in(key, 17)
    values = jax.random.truncated_normal(noise_key, -6.0, 6.0, (SLOTS, N_ROWS * TILE, TILE), jnp.float32)
    return (values * (row_scale[:, :, None] / math.sqrt(TILE))).astype(jnp.bfloat16)


def draw_row_blocks(key, part):
    return pattern_pairs(key)[0]


def draw_col_blocks(key, part):
    return pattern_pairs(key)[1]


def draw_live_counts(key, part):
    base = jax.random.fold_in(key, 11)
    first, second = jax.random.split(base)
    divisor = jax.random.randint(first, (N_BLK * N_ROWS,), 1, 5)
    counted = MAXB // divisor
    fullest = jax.random.randint(second, (), 0, N_BLK * N_ROWS)
    counted = jnp.where(jnp.arange(N_BLK * N_ROWS) == fullest, MAXB, counted)
    return counted.reshape(N_BLK, N_ROWS).astype(jnp.int32)


def steps_of(rng, shape, shards, smallest, top_value):
    gain, own = 1.0, jax.random.fold_in(rng, 6)
    for position, parts in shards:
        draws = jnp.exp(jax.random.uniform(jax.random.fold_in(own, position), (parts,), jnp.float32, smallest / len(shards), top_value / len(shards)))
        gain = gain * jnp.repeat(draws, shape[position] // parts).reshape([-1 if axis == position else 1 for axis in range(len(shape))])
    return gain


def scatter_about(own_key, extent, deviation, reach, cuts=(), kind=jnp.bfloat16):
    values = deviation * jax.random.normal(own_key, extent, jnp.float32)
    if cuts:
        values = values * steps_of(own_key, extent, cuts, -0.22, 0.18)
    return jnp.clip(values, -reach, reach).astype(kind)


def setup_inputs(seed: int = 0) -> dict:
    arg_keys = jax.random.split(jax.random.key(seed), 6)
    sens_tiles = draw_sens_tiles(jax.random.fold_in(arg_keys[5], 71), 0)
    start_basis = scatter_about(arg_keys[1], (K, CELLS), 1.0, 6.0, ((1, 8),))
    row_blocks = draw_row_blocks(jax.random.fold_in(arg_keys[5], 71), 0)
    col_blocks = draw_col_blocks(jax.random.fold_in(arg_keys[5], 71), 0)
    live_counts = draw_live_counts(jax.random.fold_in(arg_keys[5], 71), 0)
    return {"sens_tiles": sens_tiles, "start_basis": start_basis, "row_blocks": row_blocks, "col_blocks": col_blocks, "live_counts": live_counts}


def forward_one(tile_set, basis_blocks, row_slots, col_slots, count_live):
    picked = jnp.take(basis_blocks, col_slots, axis=1)
    products = jnp.einsum('kst,sit->ksi', picked, tile_set)
    live = jnp.arange(MAXB) < count_live
    onehot = ((row_slots[None, :] == jnp.arange(RB)[:, None]) & live[None, :]).astype(jnp.float32)
    summed = jnp.einsum('ksi,rs->kri', products, onehot, precision=lax.Precision.HIGHEST)
    return summed.reshape(K, RB * TILE)

def backward_one(tile_set, image_blocks, row_slots, col_slots, count_live):
    picked = jnp.take(image_blocks, row_slots, axis=1)
    products = jnp.einsum('ksi,sij->ksj', picked, tile_set)
    live = jnp.arange(MAXB) < count_live
    onehot = ((col_slots[None, :] == jnp.arange(CB)[:, None]) & live[None, :]).astype(jnp.float32)
    summed = jnp.einsum('ksj,cs->kcj', products, onehot, precision=lax.Precision.HIGHEST)
    return summed.reshape(K, CB * TILE)

def cholesky_qr(current, total):
    gram = jnp.dot(current, current.T, precision=lax.Precision.HIGHEST) / total
    lower = jnp.linalg.cholesky(gram)
    return jax.scipy.linalg.solve_triangular(lower, current, lower=True)

def reference(sens_tiles, start_basis, row_blocks, col_blocks, live_counts):
    tile_grid = sens_tiles.reshape(N_BLK, MAXB, N_ROWS, TILE, TILE)
    row_grid = row_blocks.reshape(N_BLK, MAXB, N_ROWS)
    col_grid = col_blocks.reshape(N_BLK, MAXB, N_ROWS)
    total = float(N_BLK * CB * TILE)
    basis_now = start_basis
    results = []
    for iteration in range(ITERS):
        blocks = basis_now.astype(jnp.float32).reshape(K, N_BLK, CB, TILE)

        def add_block(accum, index):
            tile_set = tile_grid[index].astype(jnp.float32)
            own = blocks[:, index]
            terms = jax.vmap(lambda place: forward_one(tile_set[:, place], own, row_grid[index, :, place], col_grid[index, :, place], live_counts[index, place]))(jnp.arange(N_ROWS))
            return (accum + terms, None)
        image, unused = lax.scan(add_block, jnp.zeros((N_ROWS, K, RB * TILE), jnp.float32), jnp.arange(N_BLK))
        image_half = image.astype(jnp.bfloat16)
        image_float = image_half.astype(jnp.float32).reshape(N_ROWS, K, RB, TILE)

        def back_block(index):
            tile_set = tile_grid[index].astype(jnp.float32)
            terms = jax.vmap(lambda place: backward_one(tile_set[:, place], image_float[place], row_grid[index, :, place], col_grid[index, :, place], live_counts[index, place]))(jnp.arange(N_ROWS))
            return jnp.sum(terms, axis=0)
        hessian = lax.map(back_block, jnp.arange(N_BLK))
        hessian = jnp.transpose(hessian, (1, 0, 2)).reshape(K, N_BLK * CB * TILE)
        result = cholesky_qr(hessian, total)
        results.append(result)
        basis_now = result.astype(jnp.bfloat16)
    return jnp.stack(results, axis=0)
```

```python
import functools

import jax
import jax.numpy as jnp
from jax import lax
from jax.experimental import pallas as pl
from jax.experimental.pallas import tpu as pltpu
from jax.sharding import PartitionSpec as P

RB = 8
CB = 32
ITERS = 4
MESH = pl.DeviceIdType.MESH
F32 = jnp.float32
BF16 = jnp.bfloat16
HIGHEST = lax.Precision.HIGHEST
CODE = jnp.int16
TOP = 32767.0


def aligned(index, width):
    return pl.ds(pl.multiple_of(index * width, width), width)


def inverse_factor(gram):
    size = gram.shape[0]
    step = 8
    shape = (step, 2 * size)
    row_id = lax.broadcasted_iota(jnp.int32, (size, size), 0)
    lane_id = lax.broadcasted_iota(jnp.int32, (size, size), 1)
    eye = (row_id == lane_id).astype(F32)
    whole = jnp.concatenate([gram, eye], axis=1)
    blocks = [whole[b * step : (b + 1) * step, :] for b in range(size // step)]
    sub_id = lax.broadcasted_iota(jnp.int32, shape, 0)

    def full(values):
        return jnp.broadcast_to(values, shape)

    outs = []
    for b in range(size // step):
        home, base = blocks[b], b * step
        cols = [full(home[:, base + k : base + k + 1]) for k in range(step)]
        entry = {(i, k): full(cols[k][i : i + 1, :]) for k in range(step) for i in range(k, step)}
        rows = [full(home[k : k + 1, :]) for k in range(step)]
        lower = {
            c: [full(blocks[c][:, base + k : base + k + 1]) for k in range(step)]
            for c in range(b + 1, size // step)
        }
        factor, inverse = {}, []
        for k in range(step):
            inverse.append(1.0 / entry[k, k])
            for i in range(k + 1, step):
                factor[i, k] = entry[i, k] * inverse[k]
            for i in range(k + 1, step):
                for j in range(k + 1, i + 1):
                    entry[i, j] = entry[i, j] - factor[i, k] * entry[j, k]
        for k in range(step):
            for i in range(k + 1, step):
                rows[i] = rows[i] - factor[i, k] * rows[k]
        out = rows[0] * lax.rsqrt(entry[0, 0])
        for k in range(1, step):
            out = jnp.where(sub_id == k, rows[k] * lax.rsqrt(entry[k, k]), out)
        outs.append(out)
        solved = [rows[k] * inverse[k] for k in range(step)]
        for k in reversed(range(step)):
            for i in range(k):
                solved[i] = solved[i] - factor[k, i] * solved[k]
        for c in range(b + 1, size // step):
            terms = [lower[c][k] * solved[k] for k in range(step)]
            while len(terms) > 1:
                terms = [terms[2 * t] + terms[2 * t + 1] for t in range(len(terms) // 2)]
            blocks[c] = blocks[c] - terms[0]
    return jnp.concatenate(outs, axis=0)[:, size:]


def diagonal_of(size):
    row_id = lax.broadcasted_iota(jnp.int32, (size, size), 0)
    return row_id == lax.broadcasted_iota(jnp.int32, (size, size), 1)


def encode(values, code_ref, scale_ref):
    size = values.shape[0]
    top = jnp.maximum(jnp.max(jnp.abs(values), axis=1, keepdims=True), 1e-30)
    code_ref[...] = jnp.round(values * (TOP / top)).astype(jnp.int32).astype(CODE)
    along = jnp.sum(jnp.where(diagonal_of(size), top * (1.0 / TOP), 0.0), axis=0, keepdims=True)
    scale_ref[:, :size] = jnp.broadcast_to(along, (8, size))
    scale_ref[:, size:] = jnp.broadcast_to(along, (8, size))


def decode(code_ref, scale_ref):
    size = code_ref.shape[0]
    along = scale_ref[0:1, :size]
    scale = jnp.sum(jnp.where(diagonal_of(size), along, 0.0), axis=1, keepdims=True)
    return code_ref[...].astype(F32) * scale


def kernel(
    n,
    m,
    total,
    inv_ref,
    tiles_hbm,
    start_ref,
    out_ref,
    tiles,
    dense,
    basis,
    part,
    rs_buf,
    half_own,
    half,
    hess_own,
    z_out,
    z_out_scale,
    z_in,
    z_in_scale,
    hz,
    hz_scale,
    gram_own,
    gram_rows,
    gram_line,
    gram_blk,
    load_sem,
    rs_send,
    rs_recv,
    ag_send,
    ag_recv,
    zc_send,
    zc_recv,
    zs_send,
    zs_recv,
    hc_send,
    hc_recv,
    hs_send,
    hs_recv,
    gr_send,
    gr_recv,
    gb_send,
    gb_recv,
):
    slots = tiles_hbm.shape[0]
    tile = tiles_hbm.shape[1]
    vectors = start_ref.shape[0]
    data = RB * tile
    cells = start_ref.shape[1]
    width = cells // m
    owners = min(n, RB)
    span = data // owners
    group = 2 if owners % 2 == 0 else 1
    groups = owners // group
    b = lax.axis_index("blk")
    z = lax.axis_index("rows")
    way = jnp.where(lax.rem(z, 2) == 0, m - 1, 1)

    load = pltpu.make_async_copy(tiles_hbm, tiles.at[pl.ds(0, slots)], load_sem)
    load.start()

    barrier = pltpu.get_barrier_semaphore()

    @pl.loop(1, n)
    def _(d):
        pl.semaphore_signal(
            barrier, inc=1, device_id={"blk": lax.rem(b + d, n)}, device_id_type=MESH
        )

    @pl.loop(1, m)
    def _(d):
        pl.semaphore_signal(
            barrier, inc=1, device_id={"rows": lax.rem(z + d, m)}, device_id_type=MESH
        )

    tiles[slots] = jnp.zeros((tile, tile), BF16)
    basis[...] = start_ref[...]
    load.wait()

    @pl.loop(0, RB)
    def _(r):
        @pl.loop(0, CB)
        def _(c):
            dense[aligned(r, tile), aligned(c, tile)] = tiles[inv_ref[r * CB + c]]

    pl.semaphore_wait(barrier, n - 1 + m - 1)

    def copy(src, dst, send_sem, recv_sem, where):
        return pltpu.make_async_remote_copy(
            src_ref=src,
            dst_ref=dst,
            send_sem=send_sem,
            recv_sem=recv_sem,
            device_id=where,
            device_id_type=MESH,
        )

    def rs_copy(dest, slot):
        return copy(
            part.at[:, aligned(dest, span)],
            rs_buf.at[slot],
            rs_send.at[dest],
            rs_recv.at[slot],
            {"blk": dest},
        )

    def ag_copy(dest, chunk):
        return copy(
            half_own,
            half.at[:, aligned(chunk, span)],
            ag_send.at[dest],
            ag_recv.at[chunk],
            {"blk": dest},
        )

    def z_copies(dest, slot):
        there = {"rows": dest}
        return (
            copy(
                z_out_scale.at[dest], z_in_scale.at[slot], zs_send.at[dest], zs_recv.at[slot], there
            ),
            copy(z_out.at[dest], z_in.at[slot], zc_send.at[dest], zc_recv.at[slot], there),
        )

    def h_copies(dest, slot):
        there = {"rows": dest}
        return (
            copy(
                hz_scale.at[slot], hz_scale.at[slot], hs_send.at[dest], hs_recv.at[slot], there
            ),
            copy(hz.at[slot], hz.at[slot], hc_send.at[dest], hc_recv.at[slot], there),
        )

    def start(copies):
        for each in copies:
            each.start()

    def wait_recv(copies):
        for each in copies:
            each.wait_recv()

    def wait_send(copies):
        for each in copies:
            each.wait_send()

    def gr_copy(dest, slot):
        return copy(
            gram_own, gram_rows.at[slot], gr_send.at[dest], gr_recv.at[slot], {"rows": dest}
        )

    def gb_copy(dest, slot):
        return copy(
            gram_line, gram_blk.at[slot], gb_send.at[dest], gb_recv.at[slot], {"blk": dest}
        )

    def backward(c):
        return jnp.dot(half[...], dense[:, aligned(c, width)], preferred_element_type=F32)

    @pl.loop(0, ITERS)
    def _(it):
        @pl.loop(0, groups)
        def _(s):
            p = lax.rem(b // group + 1 + s, groups)
            part[:, aligned(p, group * span)] = lax.dot_general(
                basis[...],
                dense[aligned(p, group * span), :],
                (((1,), (1,)), ((), ())),
                preferred_element_type=F32,
            )
            for k in range(group):
                q = p * group + k

                @pl.when(q != b)
                def _():
                    rs_copy(q, b).start()

        @pl.when(b < owners)
        def _():
            own = part[:, aligned(b, span)]

            def add(d, acc):
                src = lax.rem(b + d, n)
                rs_copy(b, src).wait_recv()
                return acc + rs_buf[src]

            own = lax.fori_loop(1, n, add, own)
            half_own[...] = own.astype(BF16)

            @pl.loop(1, n)
            def _(d):
                ag_copy(lax.rem(b + d, n), b).start()

            half[:, aligned(b, span)] = half_own[...]

        @pl.loop(0, owners)
        def _(q):
            @pl.when(q != b)
            def _():
                ag_copy(b, q).wait_recv()
                rs_copy(q, b).wait_send()

        @pl.loop(1, m)
        def _(k):
            c = lax.rem(z + way * k, m)
            encode(backward(c), z_out.at[c], z_out_scale.at[c])
            start(z_copies(c, z))

        hess_own[...] = backward(z)

        @pl.loop(1, m)
        def _(k):
            c = lax.rem(z + way * k, m)
            wait_recv(z_copies(z, c))
            hess_own[...] += decode(z_in.at[c], z_in_scale.at[c])

        hess = hess_own[...]
        gram = lax.dot_general(
            hess, hess, (((1,), (1,)), ((), ())), precision=HIGHEST, preferred_element_type=F32
        )
        fold = vectors // 2
        gram_own[...] = jnp.concatenate([gram[:fold], gram[fold:]], axis=1)

        @pl.loop(1, m)
        def _(d):
            gr_copy(lax.rem(z + d, m), z).start()

        @pl.when(it < ITERS - 1)
        def _():
            encode(hess_own[...], hz.at[z], hz_scale.at[z])

            @pl.loop(1, m)
            def _(k):
                start(h_copies(lax.rem(z + way * k, m), z))

        def add_line(d, acc):
            src = lax.rem(z + d, m)
            gr_copy(z, src).wait_recv()
            return acc + gram_rows[src]

        gram_line[...] = lax.fori_loop(1, m, add_line, gram_own[...])

        @pl.loop(1, n)
        def _(d):
            gb_copy(lax.rem(b + d, n), b).start()

        def add_blk(d, acc):
            src = lax.rem(b + d, n)
            gb_copy(b, src).wait_recv()
            return acc + gram_blk[src]

        packed = lax.fori_loop(1, n, add_blk, gram_line[...])
        gram = jnp.concatenate([packed[:, :vectors], packed[:, vectors:]], axis=0) / total

        @pl.loop(1, m)
        def _(d):
            there = lax.rem(z + d, m)
            wait_send(z_copies(there, z))
            gr_copy(there, z).wait_send()

        @pl.loop(1, n)
        def _(d):
            gb_copy(lax.rem(b + d, n), b).wait_send()

        @pl.when(b < owners)
        def _():
            @pl.loop(1, n)
            def _(d):
                ag_copy(lax.rem(b + d, n), b).wait_send()

        factor = inverse_factor(gram)
        result = jnp.dot(factor, hess_own[...], precision=HIGHEST, preferred_element_type=F32)
        basis[:, aligned(z, width)] = result.astype(BF16)
        out_ref[it] = result

        @pl.when(it < ITERS - 1)
        def _():
            @pl.loop(1, m)
            def _(k):
                c = lax.rem(z + way * k, m)
                wait_recv(h_copies(z, c))
                other = jnp.dot(
                    factor,
                    decode(hz.at[c], hz_scale.at[c]),
                    precision=HIGHEST,
                    preferred_element_type=F32,
                )
                basis[:, aligned(c, width)] = other.astype(BF16)

            @pl.loop(1, m)
            def _(k):
                wait_send(h_copies(lax.rem(z + way * k, m), z))


def local(n, m, sens_tiles, start_basis, row_blocks, col_blocks, live_counts):
    slots, tile = sens_tiles.shape[0], sens_tiles.shape[2]
    vectors, cells = start_basis.shape
    data, width = RB * tile, cells // m
    span = data // min(n, RB)
    numbers = jnp.arange(slots, dtype=jnp.int32)
    places = row_blocks[:, 0] * CB + col_blocks[:, 0]
    hit = (places[None, :] == jnp.arange(RB * CB, dtype=jnp.int32)[:, None]) & (
        numbers < live_counts[0, 0]
    )[None, :]
    inv = jnp.min(jnp.where(hit, numbers[None, :], slots), axis=1)
    total = float(cells * n)
    dma = pltpu.SemaphoreType.DMA
    return pl.pallas_call(
        functools.partial(kernel, n, m, total),
        out_shape=jax.ShapeDtypeStruct((ITERS, vectors, width), F32),
        in_specs=[
            pl.BlockSpec(memory_space=pltpu.SMEM),
            pl.BlockSpec(memory_space=pl.ANY),
            pl.BlockSpec(memory_space=pltpu.VMEM),
        ],
        out_specs=pl.BlockSpec(memory_space=pltpu.VMEM),
        scratch_shapes=[
            pltpu.VMEM((slots + 1, tile, tile), BF16),
            pltpu.VMEM((data, cells), BF16),
            pltpu.VMEM((vectors, cells), BF16),
            pltpu.VMEM((vectors, data), F32),
            pltpu.VMEM((n, vectors, span), F32),
            pltpu.VMEM((vectors, span), BF16),
            pltpu.VMEM((vectors, data), BF16),
            pltpu.VMEM((vectors, width), F32),
            pltpu.VMEM((m, vectors, width), CODE),
            pltpu.VMEM((m, 8, vectors * 2), F32),
            pltpu.VMEM((m, vectors, width), CODE),
            pltpu.VMEM((m, 8, vectors * 2), F32),
            pltpu.VMEM((m, vectors, width), CODE),
            pltpu.VMEM((m, 8, vectors * 2), F32),
            pltpu.VMEM((vectors // 2, vectors * 2), F32),
            pltpu.VMEM((m, vectors // 2, vectors * 2), F32),
            pltpu.VMEM((vectors // 2, vectors * 2), F32),
            pltpu.VMEM((n, vectors // 2, vectors * 2), F32),
            dma,
            dma((n,)),
            dma((n,)),
            dma((n,)),
            dma((n,)),
            dma((m,)),
            dma((m,)),
            dma((m,)),
            dma((m,)),
            dma((m,)),
            dma((m,)),
            dma((m,)),
            dma((m,)),
            dma((m,)),
            dma((m,)),
            dma((n,)),
            dma((n,)),
        ],
        compiler_params=pltpu.CompilerParams(
            collective_id=0, has_side_effects=True, vmem_limit_bytes=56 * 1024 * 1024
        ),
        name="subspace",
    )(inv, sens_tiles, start_basis)


def solution(mesh):
    in_specs = (
        P("blk", "rows", None),
        P(None, "blk"),
        P("blk", "rows"),
        P("blk", "rows"),
        P("blk", "rows"),
    )
    out_specs = P(None, None, ("blk", "rows"))
    return jax.shard_map(
        functools.partial(local, mesh.shape["blk"], mesh.shape["rows"]),
        mesh=mesh,
        in_specs=in_specs,
        out_specs=out_specs,
        check_vma=False,
    )
```

```python
import functools

import jax
import jax.numpy as jnp
from jax import lax
from jax.experimental import pallas as pl
from jax.experimental.pallas import tpu as pltpu
from jax.sharding import PartitionSpec as P

RB = 8
CB = 32
ITERS = 4
MESH = pl.DeviceIdType.MESH
F32 = jnp.float32
BF16 = jnp.bfloat16
HIGHEST = lax.Precision.HIGHEST
CODE = jnp.int16
TOP = 32767.0
PIECES = 1


def aligned(index, width):
    return pl.ds(pl.multiple_of(index * width, width), width)


def inverse_factor(gram):
    size = gram.shape[0]
    step = 8
    shape = (step, 2 * size)
    row_id = lax.broadcasted_iota(jnp.int32, (size, size), 0)
    lane_id = lax.broadcasted_iota(jnp.int32, (size, size), 1)
    eye = (row_id == lane_id).astype(F32)
    whole = jnp.concatenate([gram, eye], axis=1)
    blocks = [whole[b * step : (b + 1) * step, :] for b in range(size // step)]
    sub_id = lax.broadcasted_iota(jnp.int32, shape, 0)

    def full(values):
        return jnp.broadcast_to(values, shape)

    outs = []
    for b in range(size // step):
        home, base = blocks[b], b * step
        cols = [full(home[:, base + k : base + k + 1]) for k in range(step)]
        entry = {(i, k): full(cols[k][i : i + 1, :]) for k in range(step) for i in range(k, step)}
        rows = [full(home[k : k + 1, :]) for k in range(step)]
        lower = {
            c: [full(blocks[c][:, base + k : base + k + 1]) for k in range(step)]
            for c in range(b + 1, size // step)
        }
        factor, inverse = {}, []
        for k in range(step):
            inverse.append(1.0 / entry[k, k])
            for i in range(k + 1, step):
                factor[i, k] = entry[i, k] * inverse[k]
            for i in range(k + 1, step):
                for j in range(k + 1, i + 1):
                    entry[i, j] = entry[i, j] - factor[i, k] * entry[j, k]
        for k in range(step):
            for i in range(k + 1, step):
                rows[i] = rows[i] - factor[i, k] * rows[k]
        out = rows[0] * lax.rsqrt(entry[0, 0])
        for k in range(1, step):
            out = jnp.where(sub_id == k, rows[k] * lax.rsqrt(entry[k, k]), out)
        outs.append(out)
        solved = [rows[k] * inverse[k] for k in range(step)]
        for k in reversed(range(step)):
            for i in range(k):
                solved[i] = solved[i] - factor[k, i] * solved[k]
        for c in range(b + 1, size // step):
            terms = [lower[c][k] * solved[k] for k in range(step)]
            while len(terms) > 1:
                terms = [terms[2 * t] + terms[2 * t + 1] for t in range(len(terms) // 2)]
            blocks[c] = blocks[c] - terms[0]
    return jnp.concatenate(outs, axis=0)[:, size:]


def diagonal_of(size):
    row_id = lax.broadcasted_iota(jnp.int32, (size, size), 0)
    return row_id == lax.broadcasted_iota(jnp.int32, (size, size), 1)


def encode(values, code_ref, scale_ref):
    size = values.shape[0]
    top = jnp.maximum(jnp.max(jnp.abs(values), axis=1, keepdims=True), 1e-30)
    code_ref[...] = jnp.round(values * (TOP / top)).astype(jnp.int32).astype(CODE)
    along = jnp.sum(jnp.where(diagonal_of(size), top * (1.0 / TOP), 0.0), axis=0, keepdims=True)
    scale_ref[:, :size] = jnp.broadcast_to(along, (8, size))
    scale_ref[:, size:] = jnp.broadcast_to(along, (8, size))


def decode(code_ref, scale_ref):
    size = code_ref.shape[0]
    along = scale_ref[0:1, :size]
    scale = jnp.sum(jnp.where(diagonal_of(size), along, 0.0), axis=1, keepdims=True)
    return code_ref[...].astype(F32) * scale


def kernel(
    n,
    m,
    total,
    inv_ref,
    tiles_hbm,
    start_ref,
    out_ref,
    tiles,
    dense,
    basis,
    part,
    rs_buf,
    half_own,
    half,
    hess_own,
    z_out,
    z_out_scale,
    z_in,
    z_in_scale,
    mid_in,
    mid_in_scale,
    mid_sum,
    hz,
    hz_scale,
    gram_own,
    gram_rows,
    gram_line,
    gram_blk,
    load_sem,
    rs_send,
    rs_recv,
    ag_send,
    ag_recv,
    zc_send,
    zc_recv,
    zs_send,
    zs_recv,
    mc_recv,
    ms_recv,
    hc_send,
    hc_recv,
    hs_send,
    hs_recv,
    gr_send,
    gr_recv,
    gb_send,
    gb_recv,
):
    slots = tiles_hbm.shape[0]
    tile = tiles_hbm.shape[1]
    vectors = start_ref.shape[0]
    data = RB * tile
    cells = start_ref.shape[1]
    width = cells // m
    owners = min(n, RB)
    span = data // owners
    group = 2 if owners % 2 == 0 else 1
    groups = owners // group
    b = lax.axis_index("blk")
    z = lax.axis_index("rows")
    piece = width // PIECES
    outward = jnp.where(lax.rem(z, 2) == 0, m - 1, 1)
    inward = jnp.where(2 * z < m, m - 1, 1)
    near = jnp.where(z == 0, min(1, m - 1), max(m - 2, 0))

    def far(a, c):
        if m < 3:
            return jnp.bool_(False)
        return jnp.logical_or(
            jnp.logical_and(a == 0, c == m - 1), jnp.logical_and(a == m - 1, c == 0)
        )

    def merges(c):
        if m < 3:
            return jnp.bool_(False)
        return jnp.logical_or(
            jnp.logical_and(z == 1, c == m - 1), jnp.logical_and(z == m - 2, c == 0)
        )

    load = pltpu.make_async_copy(tiles_hbm, tiles.at[pl.ds(0, slots)], load_sem)
    load.start()

    barrier = pltpu.get_barrier_semaphore()

    @pl.loop(1, n)
    def _(d):
        pl.semaphore_signal(
            barrier, inc=1, device_id={"blk": lax.rem(b + d, n)}, device_id_type=MESH
        )

    @pl.loop(1, m)
    def _(d):
        pl.semaphore_signal(
            barrier, inc=1, device_id={"rows": lax.rem(z + d, m)}, device_id_type=MESH
        )

    tiles[slots] = jnp.zeros((tile, tile), BF16)
    basis[...] = start_ref[...]
    load.wait()

    @pl.loop(0, RB)
    def _(r):
        @pl.loop(0, CB)
        def _(c):
            dense[aligned(r, tile), aligned(c, tile)] = tiles[inv_ref[r * CB + c]]

    pl.semaphore_wait(barrier, n - 1 + m - 1)

    def copy(src, dst, send_sem, recv_sem, where):
        return pltpu.make_async_remote_copy(
            src_ref=src,
            dst_ref=dst,
            send_sem=send_sem,
            recv_sem=recv_sem,
            device_id=where,
            device_id_type=MESH,
        )

    def rs_copy(dest, slot):
        return copy(
            part.at[:, aligned(dest, span)],
            rs_buf.at[slot],
            rs_send.at[dest],
            rs_recv.at[slot],
            {"blk": dest},
        )

    def ag_copy(dest, chunk):
        return copy(
            half_own,
            half.at[:, aligned(chunk, span)],
            ag_send.at[dest],
            ag_recv.at[chunk],
            {"blk": dest},
        )

    def z_copies(dest, slot, p):
        there = {"rows": dest}
        k, e = dest * PIECES + p, slot * PIECES + p
        return (
            copy(z_out_scale.at[k], z_in_scale.at[e], zs_send.at[k], zs_recv.at[e], there),
            copy(z_out.at[k], z_in.at[e], zc_send.at[k], zc_recv.at[e], there),
        )

    def mid_copies(dest, side, p):
        there = {"rows": near}
        k, e = dest * PIECES + p, side * PIECES + p
        return (
            copy(z_out_scale.at[k], mid_in_scale.at[e], zs_send.at[k], ms_recv.at[e], there),
            copy(z_out.at[k], mid_in.at[e], zc_send.at[k], mc_recv.at[e], there),
        )

    def h_copies(dest, slot, p, passed=0):
        there = {"rows": dest}
        k, e = (passed * m + dest) * PIECES + p, slot * PIECES + p
        return (
            copy(hz_scale.at[e], hz_scale.at[e], hs_send.at[k], hs_recv.at[e], there),
            copy(hz.at[e], hz.at[e], hc_send.at[k], hc_recv.at[e], there),
        )

    def start(copies):
        for each in copies:
            each.start()

    def wait_recv(copies):
        for each in copies:
            each.wait_recv()

    def wait_send(copies):
        for each in copies:
            each.wait_send()

    def gr_copy(dest, slot):
        return copy(
            gram_own, gram_rows.at[slot], gr_send.at[dest], gr_recv.at[slot], {"rows": dest}
        )

    def gb_copy(dest, slot):
        return copy(
            gram_line, gram_blk.at[slot], gb_send.at[dest], gb_recv.at[slot], {"blk": dest}
        )

    def backward(c):
        return jnp.dot(half[...], dense[:, aligned(c, width)], preferred_element_type=F32)

    def backward_piece(c, p):
        return jnp.dot(
            half[...], dense[:, aligned(c * PIECES + p, piece)], preferred_element_type=F32
        )

    def cut(p):
        return slice(p * piece, (p + 1) * piece)

    def merge(side, c):
        mid_sum[...] = backward(c)
        for p in range(PIECES):
            k, e = c * PIECES + p, side * PIECES + p
            wait_recv(mid_copies(c, side, p))
            value = mid_sum[:, cut(p)] + decode(mid_in.at[e], mid_in_scale.at[e])
            encode(value, z_out.at[k], z_out_scale.at[k])
            start(z_copies(c, z, p))

    def forward_on(dest, chunk):
        for p in range(PIECES):
            wait_recv(h_copies(z, chunk, p))
            start(h_copies(dest, chunk, p, 1))

    @pl.loop(0, ITERS)
    def _(it):
        @pl.loop(0, groups)
        def _(s):
            p = lax.rem(b // group + 1 + s, groups)
            part[:, aligned(p, group * span)] = lax.dot_general(
                basis[...],
                dense[aligned(p, group * span), :],
                (((1,), (1,)), ((), ())),
                preferred_element_type=F32,
            )
            for k in range(group):
                q = p * group + k

                @pl.when(q != b)
                def _():
                    rs_copy(q, b).start()

        @pl.when(b < owners)
        def _():
            own = part[:, aligned(b, span)]

            def add(d, acc):
                src = lax.rem(b + d, n)
                rs_copy(b, src).wait_recv()
                return acc + rs_buf[src]

            own = lax.fori_loop(1, n, add, own)
            half_own[...] = own.astype(BF16)

            @pl.loop(1, n)
            def _(d):
                ag_copy(lax.rem(b + d, n), b).start()

            half[:, aligned(b, span)] = half_own[...]

        @pl.loop(0, owners)
        def _(q):
            @pl.when(q != b)
            def _():
                ag_copy(b, q).wait_recv()
                rs_copy(q, b).wait_send()

        @pl.loop(1, m)
        def _(k):
            c = lax.rem(z + outward * k, m)

            @pl.when(jnp.logical_not(merges(c)))
            def _():
                for p in range(PIECES):
                    e = c * PIECES + p
                    encode(backward_piece(c, p), z_out.at[e], z_out_scale.at[e])

                    @pl.when(far(z, c))
                    def _():
                        start(mid_copies(c, jnp.where(z == 0, 0, 1), p))

                    @pl.when(jnp.logical_not(far(z, c)))
                    def _():
                        start(z_copies(c, z, p))

        hess_own[...] = backward(z)

        if m > 2:

            @pl.when(z == 1)
            def _():
                merge(0, m - 1)

            @pl.when(z == m - 2)
            def _():
                merge(1, 0)

        @pl.loop(1, m)
        def _(k):
            c = lax.rem(z + inward * k, m)

            @pl.when(jnp.logical_not(far(z, c)))
            def _():
                for p in range(PIECES):
                    e = c * PIECES + p
                    wait_recv(z_copies(z, c, p))
                    hess_own[:, cut(p)] += decode(z_in.at[e], z_in_scale.at[e])

        hess = hess_own[...]
        gram = lax.dot_general(
            hess, hess, (((1,), (1,)), ((), ())), precision=HIGHEST, preferred_element_type=F32
        )
        fold = vectors // 2
        gram_own[...] = jnp.concatenate([gram[:fold], gram[fold:]], axis=1)

        @pl.loop(1, m)
        def _(d):
            gr_copy(lax.rem(z + d, m), z).start()

        @pl.when(it < ITERS - 1)
        def _():
            for p in range(PIECES):
                e = z * PIECES + p
                encode(hess_own[:, cut(p)], hz.at[e], hz_scale.at[e])

            @pl.loop(1, m)
            def _(k):
                c = lax.rem(z + inward * k, m)

                @pl.when(jnp.logical_not(far(z, c)))
                def _():
                    for p in range(PIECES):
                        start(h_copies(c, z, p))

        def add_line(d, acc):
            src = lax.rem(z + d, m)
            gr_copy(z, src).wait_recv()
            return acc + gram_rows[src]

        gram_line[...] = lax.fori_loop(1, m, add_line, gram_own[...])

        @pl.loop(1, n)
        def _(d):
            gb_copy(lax.rem(b + d, n), b).start()

        if m > 2:

            @pl.when(jnp.logical_and(it < ITERS - 1, z == m - 2))
            def _():
                forward_on(m - 1, 0)

            @pl.when(jnp.logical_and(it < ITERS - 1, z == 1))
            def _():
                forward_on(0, m - 1)

        def add_blk(d, acc):
            src = lax.rem(b + d, n)
            gb_copy(b, src).wait_recv()
            return acc + gram_blk[src]

        packed = lax.fori_loop(1, n, add_blk, gram_line[...])
        gram = jnp.concatenate([packed[:, :vectors], packed[:, vectors:]], axis=0) / total

        @pl.loop(1, m)
        def _(d):
            there = lax.rem(z + d, m)
            for p in range(PIECES):
                wait_send(z_copies(there, z, p))
            gr_copy(there, z).wait_send()

        @pl.loop(1, n)
        def _(d):
            gb_copy(lax.rem(b + d, n), b).wait_send()

        @pl.when(b < owners)
        def _():
            @pl.loop(1, n)
            def _(d):
                ag_copy(lax.rem(b + d, n), b).wait_send()

        factor = inverse_factor(gram)
        result = jnp.dot(factor, hess_own[...], precision=HIGHEST, preferred_element_type=F32)
        basis[:, aligned(z, width)] = result.astype(BF16)
        out_ref[it] = result

        @pl.when(it < ITERS - 1)
        def _():
            @pl.loop(1, m)
            def _(k):
                c = lax.rem(z + (m - inward) * k, m)
                passed = jnp.logical_and(m > 2, merges(c))
                for p in range(PIECES):
                    e = c * PIECES + p

                    @pl.when(jnp.logical_not(passed))
                    def _():
                        wait_recv(h_copies(z, c, p))

                    other = jnp.dot(
                        factor,
                        decode(hz.at[e], hz_scale.at[e]),
                        precision=HIGHEST,
                        preferred_element_type=F32,
                    )
                    basis[:, aligned(e, piece)] = other.astype(BF16)

            @pl.loop(1, m)
            def _(k):
                c = lax.rem(z + inward * k, m)

                @pl.when(jnp.logical_not(far(z, c)))
                def _():
                    for p in range(PIECES):
                        wait_send(h_copies(c, z, p))

            if m > 2:

                @pl.when(z == m - 2)
                def _():
                    for p in range(PIECES):
                        wait_send(h_copies(m - 1, 0, p, 1))

                @pl.when(z == 1)
                def _():
                    for p in range(PIECES):
                        wait_send(h_copies(0, m - 1, p, 1))


def local(n, m, sens_tiles, start_basis, row_blocks, col_blocks, live_counts):
    slots, tile = sens_tiles.shape[0], sens_tiles.shape[2]
    vectors, cells = start_basis.shape
    data, width = RB * tile, cells // m
    span = data // min(n, RB)
    piece = width // PIECES
    numbers = jnp.arange(slots, dtype=jnp.int32)
    places = row_blocks[:, 0] * CB + col_blocks[:, 0]
    hit = (places[None, :] == jnp.arange(RB * CB, dtype=jnp.int32)[:, None]) & (
        numbers < live_counts[0, 0]
    )[None, :]
    inv = jnp.min(jnp.where(hit, numbers[None, :], slots), axis=1)
    total = float(cells * n)
    dma = pltpu.SemaphoreType.DMA
    return pl.pallas_call(
        functools.partial(kernel, n, m, total),
        out_shape=jax.ShapeDtypeStruct((ITERS, vectors, width), F32),
        in_specs=[
            pl.BlockSpec(memory_space=pltpu.SMEM),
            pl.BlockSpec(memory_space=pl.ANY),
            pl.BlockSpec(memory_space=pltpu.VMEM),
        ],
        out_specs=pl.BlockSpec(memory_space=pltpu.VMEM),
        scratch_shapes=[
            pltpu.VMEM((slots + 1, tile, tile), BF16),
            pltpu.VMEM((data, cells), BF16),
            pltpu.VMEM((vectors, cells), BF16),
            pltpu.VMEM((vectors, data), F32),
            pltpu.VMEM((n, vectors, span), F32),
            pltpu.VMEM((vectors, span), BF16),
            pltpu.VMEM((vectors, data), BF16),
            pltpu.VMEM((vectors, width), F32),
            pltpu.VMEM((m * PIECES, vectors, piece), CODE),
            pltpu.VMEM((m * PIECES, 8, vectors * 2), F32),
            pltpu.VMEM((m * PIECES, vectors, piece), CODE),
            pltpu.VMEM((m * PIECES, 8, vectors * 2), F32),
            pltpu.VMEM((2 * PIECES, vectors, piece), CODE),
            pltpu.VMEM((2 * PIECES, 8, vectors * 2), F32),
            pltpu.VMEM((vectors, width), F32),
            pltpu.VMEM((m * PIECES, vectors, piece), CODE),
            pltpu.VMEM((m * PIECES, 8, vectors * 2), F32),
            pltpu.VMEM((vectors // 2, vectors * 2), F32),
            pltpu.VMEM((m, vectors // 2, vectors * 2), F32),
            pltpu.VMEM((vectors // 2, vectors * 2), F32),
            pltpu.VMEM((n, vectors // 2, vectors * 2), F32),
            dma,
            dma((n,)),
            dma((n,)),
            dma((n,)),
            dma((n,)),
            dma((m * PIECES,)),
            dma((m * PIECES,)),
            dma((m * PIECES,)),
            dma((m * PIECES,)),
            dma((2 * PIECES,)),
            dma((2 * PIECES,)),
            dma((2 * m * PIECES,)),
            dma((m * PIECES,)),
            dma((2 * m * PIECES,)),
            dma((m * PIECES,)),
            dma((m,)),
            dma((m,)),
            dma((n,)),
            dma((n,)),
        ],
        compiler_params=pltpu.CompilerParams(
            collective_id=0, has_side_effects=True, vmem_limit_bytes=56 * 1024 * 1024
        ),
        name="subspace",
    )(inv, sens_tiles, start_basis)


def solution(mesh):
    in_specs = (
        P("blk", "rows", None),
        P(None, "blk"),
        P("blk", "rows"),
        P("blk", "rows"),
        P("blk", "rows"),
    )
    out_specs = P(None, None, ("blk", "rows"))
    return jax.shard_map(
        functools.partial(local, mesh.shape["blk"], mesh.shape["rows"]),
        mesh=mesh,
        in_specs=in_specs,
        out_specs=out_specs,
        check_vma=False,
    )
```

```python
import functools

import jax
import jax.numpy as jnp
from jax import lax
from jax.experimental import pallas as pl
from jax.experimental.pallas import tpu as pltpu
from jax.sharding import PartitionSpec as P

RB = 8
CB = 32
ITERS = 4
MESH = pl.DeviceIdType.MESH
F32 = jnp.float32
BF16 = jnp.bfloat16
HIGHEST = lax.Precision.HIGHEST
CODE = jnp.int16
TOP = 32767.0
PIECES = 2


def aligned(index, width):
    return pl.ds(pl.multiple_of(index * width, width), width)


def inverse_factor(gram):
    size = gram.shape[0]
    step = 8
    shape = (step, 2 * size)
    row_id = lax.broadcasted_iota(jnp.int32, (size, size), 0)
    lane_id = lax.broadcasted_iota(jnp.int32, (size, size), 1)
    eye = (row_id == lane_id).astype(F32)
    whole = jnp.concatenate([gram, eye], axis=1)
    blocks = [whole[b * step : (b + 1) * step, :] for b in range(size // step)]
    sub_id = lax.broadcasted_iota(jnp.int32, shape, 0)

    def full(values):
        return jnp.broadcast_to(values, shape)

    outs = []
    for b in range(size // step):
        home, base = blocks[b], b * step
        cols = [full(home[:, base + k : base + k + 1]) for k in range(step)]
        entry = {(i, k): full(cols[k][i : i + 1, :]) for k in range(step) for i in range(k, step)}
        rows = [full(home[k : k + 1, :]) for k in range(step)]
        lower = {
            c: [full(blocks[c][:, base + k : base + k + 1]) for k in range(step)]
            for c in range(b + 1, size // step)
        }
        factor, inverse = {}, []
        for k in range(step):
            inverse.append(1.0 / entry[k, k])
            for i in range(k + 1, step):
                factor[i, k] = entry[i, k] * inverse[k]
            for i in range(k + 1, step):
                for j in range(k + 1, i + 1):
                    entry[i, j] = entry[i, j] - factor[i, k] * entry[j, k]
        for k in range(step):
            for i in range(k + 1, step):
                rows[i] = rows[i] - factor[i, k] * rows[k]
        out = rows[0] * lax.rsqrt(entry[0, 0])
        for k in range(1, step):
            out = jnp.where(sub_id == k, rows[k] * lax.rsqrt(entry[k, k]), out)
        outs.append(out)
        solved = [rows[k] * inverse[k] for k in range(step)]
        for k in reversed(range(step)):
            for i in range(k):
                solved[i] = solved[i] - factor[k, i] * solved[k]
        for c in range(b + 1, size // step):
            terms = [lower[c][k] * solved[k] for k in range(step)]
            while len(terms) > 1:
                terms = [terms[2 * t] + terms[2 * t + 1] for t in range(len(terms) // 2)]
            blocks[c] = blocks[c] - terms[0]
    return jnp.concatenate(outs, axis=0)[:, size:]


def diagonal_of(size):
    row_id = lax.broadcasted_iota(jnp.int32, (size, size), 0)
    return row_id == lax.broadcasted_iota(jnp.int32, (size, size), 1)


def across(column):
    size = column.shape[0]
    return jnp.sum(jnp.where(diagonal_of(size), column, 0.0), axis=0, keepdims=True)


def down(row):
    size = row.shape[1]
    return jnp.sum(jnp.where(diagonal_of(size), row, 0.0), axis=1, keepdims=True)


def peak(values):
    return jnp.maximum(jnp.max(jnp.abs(values), axis=1, keepdims=True), 1e-30)


def put_scale(top, scale_ref):
    size = top.shape[0]
    along = across(top * (1.0 / TOP))
    scale_ref[:, :size] = jnp.broadcast_to(along, (8, size))
    scale_ref[:, size:] = jnp.broadcast_to(along, (8, size))


def get_scale(scale_ref):
    return down(scale_ref[0:1, : scale_ref.shape[1] // 2])


def to_code(values):
    return jnp.round(values).astype(jnp.int32).astype(CODE)


def table(m, z, rows):
    def pick(k):
        value = jnp.int32(0)
        for i in range(m):
            if k < len(rows[i]):
                value = jnp.where(z == i, rows[i][k], value)
        return value

    return [pick(k) for k in range(max(len(row) for row in rows))]


def orders(m):
    outgoing, incoming, shared = [], [], []
    for a in range(m):
        others = sorted((c for c in range(m) if c != a), key=lambda c: -abs(c - a))
        far = {0: m - 1, m - 1: 0}.get(a) if m > 2 else None
        merged = [m - 1] if m > 2 and a == 1 else []
        merged += [0] if m > 2 and a == m - 2 else []
        outgoing.append([c for c in others if c not in merged] + merged)
        late = {1: 0, m - 2: m - 1}.get(a)
        nearest = [c for c in reversed(others) if c != far]
        incoming.append(sorted(nearest, key=lambda c: c == late))
        shared.append([c for c in others if c != far])
    return outgoing, incoming, shared


def kernel(
    n,
    m,
    total,
    inv_ref,
    tiles_hbm,
    start_ref,
    out_ref,
    tiles,
    dense,
    turned,
    split,
    factor,
    part,
    rs_buf,
    half_own,
    half,
    hess_own,
    z_out,
    z_out_scale,
    z_in,
    z_in_scale,
    mid_sum,
    hz,
    hz_scale,
    gram_own,
    gram_rows,
    gram_line,
    gram_blk,
    load_sem,
    rs_send,
    rs_recv,
    ag_send,
    ag_recv,
    zc_send,
    zc_recv,
    zs_send,
    zs_recv,
    hc_send,
    hc_recv,
    hs_send,
    hs_recv,
    gr_send,
    gr_recv,
    gb_send,
    gb_recv,
):
    slots = tiles_hbm.shape[0]
    tile = tiles_hbm.shape[1]
    vectors = start_ref.shape[0]
    data = RB * tile
    cells = start_ref.shape[1]
    width = cells // m
    owners = min(n, RB)
    span = data // owners
    group = 2 if owners % 2 == 0 else 1
    groups = owners // group
    b = lax.axis_index("blk")
    z = lax.axis_index("rows")
    piece = width // PIECES
    outgoing, incoming, shared = (table(m, z, rows) for rows in orders(m))
    sends = m - 1 if m < 3 else (0 if m == 3 else m - 2)
    takes = m - 1 if m < 3 else m - 2
    near = jnp.where(z == 0, min(1, m - 1), max(m - 2, 0))
    at_end = jnp.logical_or(z == 0, z == m - 1)
    at_merge = jnp.logical_or(z == 1, z == m - 2)

    def far(a, c):
        if m < 3:
            return jnp.bool_(False)
        return jnp.logical_or(
            jnp.logical_and(a == 0, c == m - 1), jnp.logical_and(a == m - 1, c == 0)
        )

    def merges(c):
        if m < 3:
            return jnp.bool_(False)
        return jnp.logical_or(
            jnp.logical_and(z == 1, c == m - 1), jnp.logical_and(z == m - 2, c == 0)
        )

    load = pltpu.make_async_copy(tiles_hbm, tiles.at[pl.ds(0, slots)], load_sem)
    load.start()

    barrier = pltpu.get_barrier_semaphore()

    @pl.loop(1, n)
    def _(d):
        pl.semaphore_signal(
            barrier, inc=1, device_id={"blk": lax.rem(b + d, n)}, device_id_type=MESH
        )

    @pl.loop(1, m)
    def _(d):
        pl.semaphore_signal(
            barrier, inc=1, device_id={"rows": lax.rem(z + d, m)}, device_id_type=MESH
        )

    tiles[slots] = jnp.zeros((tile, tile), BF16)
    factor[...] = diagonal_of(vectors).astype(F32)
    load.wait()

    @pl.loop(0, RB)
    def _(r):
        @pl.loop(0, CB, unroll=4)
        def _(c):
            dense[aligned(r, tile), aligned(c, tile)] = tiles[inv_ref[r * CB + c]]

    pl.semaphore_wait(barrier, n - 1 + m - 1)

    here = lax.rem(b // group, groups)
    if groups == 4:
        visits = [3 - here, lax.rem(here + 2, 4), here + 1 - 2 * lax.rem(here, 2), here]
    else:
        visits = [lax.rem(here + 1 + s, groups) for s in range(groups)]

    def sum_over(count, init, term):
        if count > 8:
            return lax.fori_loop(1, count, term, init)
        for d in range(1, count):
            init = term(d, init)
        return init

    def copy(src, dst, send_sem, recv_sem, where):
        return pltpu.make_async_remote_copy(
            src_ref=src,
            dst_ref=dst,
            send_sem=send_sem,
            recv_sem=recv_sem,
            device_id=where,
            device_id_type=MESH,
        )

    def rs_copy(dest, slot):
        return copy(
            part.at[:, aligned(dest, span)],
            rs_buf.at[slot],
            rs_send.at[dest],
            rs_recv.at[slot],
            {"blk": dest},
        )

    def ag_copy(dest, chunk):
        return copy(
            half_own,
            half.at[:, aligned(chunk, span)],
            ag_send.at[dest],
            ag_recv.at[chunk],
            {"blk": dest},
        )

    def z_scale(dest, chunk, slot):
        return copy(
            z_out_scale.at[chunk],
            z_in_scale.at[slot],
            zs_send.at[chunk],
            zs_recv.at[slot],
            {"rows": dest},
        )

    def z_codes(dest, chunk, slot, p):
        k, e = chunk * PIECES + p, slot * PIECES + p
        return copy(z_out.at[k], z_in.at[e], zc_send.at[k], zc_recv.at[e], {"rows": dest})

    def h_scale(dest, slot, passed=0):
        k = passed * m + dest
        return copy(
            hz_scale.at[slot],
            hz_scale.at[slot],
            hs_send.at[k],
            hs_recv.at[slot],
            {"rows": dest},
        )

    def h_codes(dest, slot, p, passed=0):
        k, e = (passed * m + dest) * PIECES + p, slot * PIECES + p
        return copy(hz.at[e], hz.at[e], hc_send.at[k], hc_recv.at[e], {"rows": dest})

    def gr_copy(dest, slot):
        return copy(
            gram_own, gram_rows.at[slot], gr_send.at[dest], gr_recv.at[slot], {"rows": dest}
        )

    def gb_copy(dest, slot, turn):
        return copy(
            gram_line,
            gram_blk.at[turn, slot],
            gb_send.at[dest],
            gb_recv.at[turn, slot],
            {"blk": dest},
        )

    def backward(c):
        return jnp.dot(half[...], dense[:, aligned(c, width)], preferred_element_type=F32)

    def cut(p):
        return slice(p * piece, (p + 1) * piece)

    def send_sum(k):
        c = outgoing[k]
        value = backward(c)
        top = peak(value)
        put_scale(top, z_out_scale.at[c])
        away = far(z, c)
        dest = jnp.where(away, near, c)
        slot = jnp.where(away, jnp.where(z == 0, m, m + 1), z)
        z_scale(dest, c, slot).start()
        gain = TOP / top
        for p in range(PIECES):
            z_out[c * PIECES + p] = to_code(value[:, cut(p)] * gain)
            if k == 0:
                z_codes(dest, c, slot, p).start()
        return dest, c, slot

    def send_codes(dest, c, slot):
        for p in range(PIECES):
            z_codes(dest, c, slot, p).start()

    def merge(side, c):
        value = backward(c)
        own_top = peak(value)
        slot = m + side
        z_scale(c, c, slot).wait_recv()
        step = get_scale(z_in_scale.at[slot])
        top = step * TOP + own_top
        put_scale(top, z_out_scale.at[c])
        z_scale(c, c, z).start()
        gain = TOP / top
        mid_sum[...] = value * gain
        step = step * gain
        for p in range(PIECES):
            z_codes(c, c, slot, p).wait_recv()
            code = z_in[slot * PIECES + p].astype(F32)
            z_out[c * PIECES + p] = to_code(mid_sum[:, cut(p)] + code * step)
            z_codes(c, c, z, p).start()

    def finish(count, more):
        own_top = peak(hess_own[...])
        steps = []
        for c in incoming[:count]:
            z_scale(z, z, c).wait_recv()
            steps.append(get_scale(z_in_scale.at[c]))
        top = own_top
        for step in steps:
            top = top + step * TOP
        put_scale(top, hz_scale.at[z])

        @pl.when(more)
        def _():
            for c in shared[:count]:
                h_scale(c, z).start()

        gain = TOP / top
        for p in range(PIECES):
            value = hess_own[:, cut(p)]
            for c, step in zip(incoming[:count], steps):
                z_codes(z, z, c, p).wait_recv()
                value = value + z_in[c * PIECES + p].astype(F32) * step
            hess_own[:, cut(p)] = value
            hz[z * PIECES + p] = to_code(value * gain)

            @pl.when(more)
            def _():
                for c in shared[:count]:
                    h_codes(c, z, p).start()

    def expand(c):
        for p in range(PIECES):
            code = hz[c * PIECES + p].astype(jnp.int32)
            upper = lax.shift_right_arithmetic(code, 8)
            split[:vectors, cut(p)] = upper.astype(F32).astype(BF16)
            split[vectors:, cut(p)] = (code & 255).astype(F32).astype(BF16)

    def partial_image(c, columns):
        both = jnp.dot(
            split[...], turned[aligned(c, width), columns], preferred_element_type=F32
        )
        step = get_scale(hz_scale.at[c])
        return (both[:vectors] * 256.0 + both[vectors:]) * step

    def arrive(c):
        h_scale(z, c).wait_recv()
        for p in range(PIECES):
            h_codes(z, c, p).wait_recv()

    def pass_on(dest, chunk):
        h_scale(z, chunk).wait_recv()
        h_scale(dest, chunk, 1).start()
        for p in range(PIECES):
            h_codes(z, chunk, p).wait_recv()
            h_codes(dest, chunk, p, 1).start()

    def passed_sent(dest, chunk):
        h_scale(dest, chunk, 1).wait_send()
        for p in range(PIECES):
            h_codes(dest, chunk, p, 1).wait_send()

    def send_group(p, last):
        for k in range(group):
            q = p * group + k
            if last:

                @pl.when(q != b)
                def _():
                    rs_copy(q, b).start()

            else:
                rs_copy(q, b).start()

    @pl.loop(0, groups)
    def _(s):
        p = lax.rem(b // group + 1 + s, groups)
        part[:, aligned(p, group * span)] = lax.dot_general(
            start_ref[...],
            dense[aligned(p, group * span), :],
            (((1,), (1,)), ((), ())),
            preferred_element_type=F32,
        )
        send_group(p, True)

    def settle_blk():
        @pl.loop(1, n)
        def _(d):
            gb_copy(lax.rem(b + d, n), b, 0).wait_send()

    def settle_rows():
        def shared_sent(c):
            h_scale(c, z).wait_send()
            for p in range(PIECES):
                h_codes(c, z, p).wait_send()

        for k in range(takes):
            shared_sent(shared[k])

        if takes < m - 1:

            @pl.when(jnp.logical_not(at_end))
            def _():
                shared_sent(shared[m - 2])

            @pl.when(z == m - 2)
            def _():
                passed_sent(m - 1, 0)

            @pl.when(z == 1)
            def _():
                passed_sent(0, m - 1)

    @pl.loop(0, ITERS)
    def _(it):
        more = it < ITERS - 1
        turn = lax.rem(it, 2)

        @pl.when(it > 0)
        def _():
            settle_blk()
            settle_rows()

        @pl.when(b < owners)
        def _():
            own = part[:, aligned(b, span)]

            def add(d, acc):
                src = lax.rem(b + d, n)
                rs_copy(b, src).wait_recv()
                return acc + rs_buf[src]

            own = sum_over(n, own, add)
            own = jnp.dot(factor[...], own, precision=HIGHEST, preferred_element_type=F32)
            half_own[...] = own.astype(BF16)

            @pl.loop(1, n)
            def _(d):
                ag_copy(lax.rem(b + d, n), b).start()

            half[:, aligned(b, span)] = half_own[...]

        @pl.loop(0, owners)
        def _(q):
            @pl.when(q != b)
            def _():
                ag_copy(b, q).wait_recv()

        held = [send_sum(k) for k in range(sends)]
        hess_own[...] = backward(z)
        for each in held[1:]:
            send_codes(*each)

        if sends < m - 1:

            @pl.when(jnp.logical_not(at_merge))
            def _():
                for k in range(sends, m - 1):
                    each = send_sum(k)
                    if k > 0:
                        send_codes(*each)

            @pl.when(z == 1)
            def _():
                merge(0, m - 1)

            @pl.when(z == m - 2)
            def _():
                merge(1, 0)

        @pl.loop(0, owners)
        def _(q):
            @pl.when(q != b)
            def _():
                rs_copy(q, b).wait_send()

        @pl.when(b < owners)
        def _():
            @pl.loop(1, n)
            def _(d):
                ag_copy(lax.rem(b + d, n), b).wait_send()

        @pl.when(it == 0)
        def _():
            @pl.loop(0, RB)
            def _(r):
                for c in range(CB):
                    turned[c * tile : (c + 1) * tile, aligned(r, tile)] = dense[
                        aligned(r, tile), c * tile : (c + 1) * tile
                    ].T

        @pl.when(at_end)
        def _():
            finish(takes, more)

        if m > 2:

            @pl.when(jnp.logical_not(at_end))
            def _():
                finish(m - 1, more)

        hess = hess_own[...]
        gram = lax.dot_general(
            hess, hess, (((1,), (1,)), ((), ())), precision=HIGHEST, preferred_element_type=F32
        )
        fold = vectors // 2
        gram_own[...] = jnp.concatenate([gram[:fold], gram[fold:]], axis=1)

        @pl.loop(1, m)
        def _(d):
            gr_copy(lax.rem(z + d, m), z).start()

        @pl.when(more)
        def _():
            expand(z)
            part[...] = partial_image(z, slice(None))

        def add_line(d, acc):
            src = lax.rem(z + d, m)
            gr_copy(z, src).wait_recv()
            return acc + gram_rows[src]

        gram_line[...] = sum_over(m, gram_own[...], add_line)

        @pl.loop(1, n)
        def _(d):
            gb_copy(lax.rem(b + d, n), b, turn).start()

        if m > 2:

            @pl.when(jnp.logical_and(more, z == m - 2))
            def _():
                pass_on(m - 1, 0)

            @pl.when(jnp.logical_and(more, z == 1))
            def _():
                pass_on(0, m - 1)

        @pl.loop(1, m)
        def _(d):
            there = lax.rem(z + d, m)
            gr_copy(there, z).wait_send()
            z_scale(there, there, z).wait_send()
            for p in range(PIECES):
                z_codes(there, there, z, p).wait_send()

        @pl.when(more)
        def _():
            arrivals = outgoing[::-1]
            for k, c in enumerate(arrivals):

                @pl.when(jnp.logical_not(merges(c)))
                def _():
                    arrive(c)

                expand(c)
                if k < m - 2:
                    part[...] += partial_image(c, slice(None))
                else:
                    for p in visits:
                        columns = aligned(p, group * span)
                        part[:, columns] += partial_image(c, columns)
                        send_group(p, p is visits[-1])

        def add_blk(d, acc):
            src = lax.rem(b + d, n)
            gb_copy(b, src, turn).wait_recv()
            return acc + gram_blk[turn, src]

        packed = sum_over(n, gram_line[...], add_blk)
        gram = jnp.concatenate([packed[:, :vectors], packed[:, vectors:]], axis=0) / total
        solved = inverse_factor(gram)
        factor[...] = solved
        out_ref[it] = jnp.dot(
            solved, hess_own[...], precision=HIGHEST, preferred_element_type=F32
        )

    settle_blk()


def local(n, m, sens_tiles, start_basis, row_blocks, col_blocks, live_counts):
    slots, tile = sens_tiles.shape[0], sens_tiles.shape[2]
    vectors, cells = start_basis.shape
    data, width = RB * tile, cells // m
    span = data // min(n, RB)
    piece = width // PIECES
    numbers = jnp.arange(slots, dtype=jnp.int32)
    places = row_blocks[:, 0] * CB + col_blocks[:, 0]
    hit = (places[None, :] == jnp.arange(RB * CB, dtype=jnp.int32)[:, None]) & (
        numbers < live_counts[0, 0]
    )[None, :]
    inv = jnp.min(jnp.where(hit, numbers[None, :], slots), axis=1)
    total = float(cells * n)
    dma = pltpu.SemaphoreType.DMA
    return pl.pallas_call(
        functools.partial(kernel, n, m, total),
        out_shape=jax.ShapeDtypeStruct((ITERS, vectors, width), F32),
        in_specs=[
            pl.BlockSpec(memory_space=pltpu.SMEM),
            pl.BlockSpec(memory_space=pl.ANY),
            pl.BlockSpec(memory_space=pltpu.VMEM),
        ],
        out_specs=pl.BlockSpec(memory_space=pltpu.VMEM),
        scratch_shapes=[
            pltpu.VMEM((slots + 1, tile, tile), BF16),
            pltpu.VMEM((data, cells), BF16),
            pltpu.VMEM((cells, data), BF16),
            pltpu.VMEM((vectors * 2, width), BF16),
            pltpu.VMEM((vectors, vectors), F32),
            pltpu.VMEM((vectors, data), F32),
            pltpu.VMEM((n, vectors, span), F32),
            pltpu.VMEM((vectors, span), BF16),
            pltpu.VMEM((vectors, data), BF16),
            pltpu.VMEM((vectors, width), F32),
            pltpu.VMEM((m * PIECES, vectors, piece), CODE),
            pltpu.VMEM((m, 8, vectors * 2), F32),
            pltpu.VMEM(((m + 2) * PIECES, vectors, piece), CODE),
            pltpu.VMEM((m + 2, 8, vectors * 2), F32),
            pltpu.VMEM((vectors, width), F32),
            pltpu.VMEM((m * PIECES, vectors, piece), CODE),
            pltpu.VMEM((m, 8, vectors * 2), F32),
            pltpu.VMEM((vectors // 2, vectors * 2), F32),
            pltpu.VMEM((m, vectors // 2, vectors * 2), F32),
            pltpu.VMEM((vectors // 2, vectors * 2), F32),
            pltpu.VMEM((2, n, vectors // 2, vectors * 2), F32),
            dma,
            dma((n,)),
            dma((n,)),
            dma((n,)),
            dma((n,)),
            dma((m * PIECES,)),
            dma(((m + 2) * PIECES,)),
            dma((m,)),
            dma((m + 2,)),
            dma((2 * m * PIECES,)),
            dma((m * PIECES,)),
            dma((2 * m,)),
            dma((m,)),
            dma((m,)),
            dma((m,)),
            dma((n,)),
            dma((2, n)),
        ],
        compiler_params=pltpu.CompilerParams(
            collective_id=0, has_side_effects=True, vmem_limit_bytes=56 * 1024 * 1024
        ),
        name="subspace",
    )(inv, sens_tiles, start_basis)


def solution(mesh):
    in_specs = (
        P("blk", "rows", None),
        P(None, "blk"),
        P("blk", "rows"),
        P("blk", "rows"),
        P("blk", "rows"),
    )
    out_specs = P(None, None, ("blk", "rows"))
    return jax.shard_map(
        functools.partial(local, mesh.shape["blk"], mesh.shape["rows"]),
        mesh=mesh,
        in_specs=in_specs,
        out_specs=out_specs,
        check_vma=False,
    )
```

```python
import functools

import jax
import jax.numpy as jnp
from jax import lax
from jax.experimental import pallas as pl
from jax.experimental.pallas import tpu as pltpu
from jax.sharding import PartitionSpec as P

RB = 8
CB = 32
ITERS = 4
MESH = pl.DeviceIdType.MESH
F32 = jnp.float32
BF16 = jnp.bfloat16
HIGHEST = lax.Precision.HIGHEST
CODE = jnp.int16
TOP = 32767.0
PIECES = 2


def aligned(index, width):
    return pl.ds(pl.multiple_of(index * width, width), width)


def inverse_factor(gram):
    size = gram.shape[0]
    step = 8
    shape = (step, 2 * size)
    row_id = lax.broadcasted_iota(jnp.int32, (size, size), 0)
    lane_id = lax.broadcasted_iota(jnp.int32, (size, size), 1)
    eye = (row_id == lane_id).astype(F32)
    whole = jnp.concatenate([gram, eye], axis=1)
    blocks = [whole[b * step : (b + 1) * step, :] for b in range(size // step)]
    sub_id = lax.broadcasted_iota(jnp.int32, shape, 0)

    def full(values):
        return jnp.broadcast_to(values, shape)

    outs = []
    for b in range(size // step):
        home, base = blocks[b], b * step
        cols = [full(home[:, base + k : base + k + 1]) for k in range(step)]
        entry = {(i, k): full(cols[k][i : i + 1, :]) for k in range(step) for i in range(k, step)}
        rows = [full(home[k : k + 1, :]) for k in range(step)]
        lower = {
            c: [full(blocks[c][:, base + k : base + k + 1]) for k in range(step)]
            for c in range(b + 1, size // step)
        }
        factor, inverse = {}, []
        for k in range(step):
            inverse.append(1.0 / entry[k, k])
            for i in range(k + 1, step):
                factor[i, k] = entry[i, k] * inverse[k]
            for i in range(k + 1, step):
                for j in range(k + 1, i + 1):
                    entry[i, j] = entry[i, j] - factor[i, k] * entry[j, k]
        for k in range(step):
            for i in range(k + 1, step):
                rows[i] = rows[i] - factor[i, k] * rows[k]
        out = rows[0] * lax.rsqrt(entry[0, 0])
        for k in range(1, step):
            out = jnp.where(sub_id == k, rows[k] * lax.rsqrt(entry[k, k]), out)
        outs.append(out)
        solved = [rows[k] * inverse[k] for k in range(step)]
        for k in reversed(range(step)):
            for i in range(k):
                solved[i] = solved[i] - factor[k, i] * solved[k]
        for c in range(b + 1, size // step):
            terms = [lower[c][k] * solved[k] for k in range(step)]
            while len(terms) > 1:
                terms = [terms[2 * t] + terms[2 * t + 1] for t in range(len(terms) // 2)]
            blocks[c] = blocks[c] - terms[0]
    return jnp.concatenate(outs, axis=0)[:, size:]


def diagonal_of(size):
    row_id = lax.broadcasted_iota(jnp.int32, (size, size), 0)
    return row_id == lax.broadcasted_iota(jnp.int32, (size, size), 1)


def across(column):
    size = column.shape[0]
    return jnp.sum(jnp.where(diagonal_of(size), column, 0.0), axis=0, keepdims=True)


def down(row):
    size = row.shape[1]
    return jnp.sum(jnp.where(diagonal_of(size), row, 0.0), axis=1, keepdims=True)


def peak(values):
    return jnp.maximum(jnp.max(jnp.abs(values), axis=1, keepdims=True), 1e-30)


def put_scale(top, scale_ref):
    size = top.shape[0]
    along = across(top * (1.0 / TOP))
    scale_ref[:, :size] = jnp.broadcast_to(along, (8, size))
    scale_ref[:, size:] = jnp.broadcast_to(along, (8, size))


def get_scale(scale_ref):
    return down(scale_ref[0:1, : scale_ref.shape[1] // 2])


def to_code(values):
    return jnp.round(values).astype(jnp.int32).astype(CODE)


def table(m, z, rows):
    def pick(k):
        value = jnp.int32(0)
        for i in range(m):
            if k < len(rows[i]):
                value = jnp.where(z == i, rows[i][k], value)
        return value

    return [pick(k) for k in range(max(len(row) for row in rows))]


def orders(m):
    outgoing, incoming, shared = [], [], []
    for a in range(m):
        others = sorted((c for c in range(m) if c != a), key=lambda c: -abs(c - a))
        far = {0: m - 1, m - 1: 0}.get(a) if m > 2 else None
        merged = [m - 1] if m > 2 and a == 1 else []
        merged += [0] if m > 2 and a == m - 2 else []
        outgoing.append([c for c in others if c not in merged] + merged)
        late = {1: 0, m - 2: m - 1}.get(a)
        nearest = [c for c in reversed(others) if c != far]
        incoming.append(sorted(nearest, key=lambda c: c == late))
        shared.append([c for c in others if c != far])
    return outgoing, incoming, shared


def kernel(
    n,
    m,
    total,
    inv_ref,
    tiles_hbm,
    start_ref,
    out_ref,
    tiles,
    dense,
    turned,
    split,
    factor,
    part,
    rs_buf,
    half_own,
    half,
    hess_own,
    z_out,
    z_out_scale,
    z_in,
    z_in_scale,
    mid_sum,
    hz,
    hz_scale,
    gram_own,
    gram_rows,
    gram_line,
    gram_blk,
    load_sem,
    rs_send,
    rs_recv,
    ag_send,
    ag_recv,
    zc_send,
    zc_recv,
    zs_send,
    zs_recv,
    hc_send,
    hc_recv,
    hs_send,
    hs_recv,
    gr_send,
    gr_recv,
    gb_send,
    gb_recv,
):
    slots = tiles_hbm.shape[0]
    tile = tiles_hbm.shape[1]
    vectors = start_ref.shape[0]
    data = RB * tile
    cells = start_ref.shape[1]
    width = cells // m
    owners = min(n, RB)
    span = data // owners
    group = 2 if owners % 2 == 0 else 1
    groups = owners // group
    b = lax.axis_index("blk")
    z = lax.axis_index("rows")
    piece = width // PIECES
    outgoing, incoming, shared = (table(m, z, rows) for rows in orders(m))
    sends = m - 1 if m < 3 else (0 if m == 3 else m - 2)
    takes = m - 1 if m < 3 else m - 2
    near = jnp.where(z == 0, min(1, m - 1), max(m - 2, 0))
    at_end = jnp.logical_or(z == 0, z == m - 1)
    at_merge = jnp.logical_or(z == 1, z == m - 2)

    def far(a, c):
        if m < 3:
            return jnp.bool_(False)
        return jnp.logical_or(
            jnp.logical_and(a == 0, c == m - 1), jnp.logical_and(a == m - 1, c == 0)
        )

    def merges(c):
        if m < 3:
            return jnp.bool_(False)
        return jnp.logical_or(
            jnp.logical_and(z == 1, c == m - 1), jnp.logical_and(z == m - 2, c == 0)
        )

    load = pltpu.make_async_copy(tiles_hbm, tiles.at[pl.ds(0, slots)], load_sem)
    load.start()

    barrier = pltpu.get_barrier_semaphore()

    @pl.loop(1, n)
    def _(d):
        pl.semaphore_signal(
            barrier, inc=1, device_id={"blk": lax.rem(b + d, n)}, device_id_type=MESH
        )

    @pl.loop(1, m)
    def _(d):
        pl.semaphore_signal(
            barrier, inc=1, device_id={"rows": lax.rem(z + d, m)}, device_id_type=MESH
        )

    tiles[slots] = jnp.zeros((tile, tile), BF16)
    factor[...] = diagonal_of(vectors).astype(F32)
    load.wait()

    @pl.loop(0, RB)
    def _(r):
        @pl.loop(0, CB, unroll=4)
        def _(c):
            dense[aligned(r, tile), aligned(c, tile)] = tiles[inv_ref[r * CB + c]]

    pl.semaphore_wait(barrier, n - 1 + m - 1)

    here = lax.rem(b // group, groups)
    if groups == 4:
        visits = [3 - here, lax.rem(here + 2, 4), here + 1 - 2 * lax.rem(here, 2), here]
    else:
        visits = [lax.rem(here + 1 + s, groups) for s in range(groups)]

    def sum_over(count, init, term):
        if count > 8:
            return lax.fori_loop(1, count, term, init)
        for d in range(1, count):
            init = term(d, init)
        return init

    def copy(src, dst, send_sem, recv_sem, where):
        return pltpu.make_async_remote_copy(
            src_ref=src,
            dst_ref=dst,
            send_sem=send_sem,
            recv_sem=recv_sem,
            device_id=where,
            device_id_type=MESH,
        )

    def rs_copy(dest, slot):
        return copy(
            part.at[:, aligned(dest, span)],
            rs_buf.at[slot],
            rs_send.at[dest],
            rs_recv.at[slot],
            {"blk": dest},
        )

    def ag_copy(dest, chunk):
        return copy(
            half_own,
            half.at[:, aligned(chunk, span)],
            ag_send.at[dest],
            ag_recv.at[chunk],
            {"blk": dest},
        )

    def z_scale(dest, chunk, slot):
        return copy(
            z_out_scale.at[chunk],
            z_in_scale.at[slot],
            zs_send.at[chunk],
            zs_recv.at[slot],
            {"rows": dest},
        )

    def z_codes(dest, chunk, slot, p):
        k, e = chunk * PIECES + p, slot * PIECES + p
        return copy(z_out.at[k], z_in.at[e], zc_send.at[k], zc_recv.at[e], {"rows": dest})

    def h_scale(dest, slot, passed=0):
        k = passed * m + dest
        return copy(
            hz_scale.at[slot],
            hz_scale.at[slot],
            hs_send.at[k],
            hs_recv.at[slot],
            {"rows": dest},
        )

    def h_codes(dest, slot, p, passed=0):
        k, e = (passed * m + dest) * PIECES + p, slot * PIECES + p
        return copy(hz.at[e], hz.at[e], hc_send.at[k], hc_recv.at[e], {"rows": dest})

    def gr_copy(dest, slot):
        return copy(
            gram_line, gram_rows.at[slot], gr_send.at[dest], gr_recv.at[slot], {"rows": dest}
        )

    def gb_copy(dest, slot, turn):
        return copy(
            gram_own,
            gram_blk.at[turn, slot],
            gb_send.at[dest],
            gb_recv.at[turn, slot],
            {"blk": dest},
        )

    def backward(c):
        return jnp.dot(half[...], dense[:, aligned(c, width)], preferred_element_type=F32)

    def cut(p):
        return slice(p * piece, (p + 1) * piece)

    def send_sum(k):
        c = outgoing[k]
        value = backward(c)
        top = peak(value)
        put_scale(top, z_out_scale.at[c])
        away = far(z, c)
        dest = jnp.where(away, near, c)
        slot = jnp.where(away, jnp.where(z == 0, m, m + 1), z)
        z_scale(dest, c, slot).start()
        gain = TOP / top
        for p in range(PIECES):
            z_out[c * PIECES + p] = to_code(value[:, cut(p)] * gain)
            if k == 0:
                z_codes(dest, c, slot, p).start()
        return dest, c, slot

    def send_codes(dest, c, slot):
        for p in range(PIECES):
            z_codes(dest, c, slot, p).start()

    def merge(side, c):
        value = backward(c)
        own_top = peak(value)
        slot = m + side
        z_scale(c, c, slot).wait_recv()
        step = get_scale(z_in_scale.at[slot])
        top = step * TOP + own_top
        put_scale(top, z_out_scale.at[c])
        z_scale(c, c, z).start()
        gain = TOP / top
        mid_sum[...] = value * gain
        step = step * gain
        for p in range(PIECES):
            z_codes(c, c, slot, p).wait_recv()
            code = z_in[slot * PIECES + p].astype(F32)
            z_out[c * PIECES + p] = to_code(mid_sum[:, cut(p)] + code * step)
            z_codes(c, c, z, p).start()

    def finish(count, more):
        own_top = peak(hess_own[...])
        steps = []
        for c in incoming[:count]:
            z_scale(z, z, c).wait_recv()
            steps.append(get_scale(z_in_scale.at[c]))
        top = own_top
        for step in steps:
            top = top + step * TOP
        put_scale(top, hz_scale.at[z])

        @pl.when(more)
        def _():
            for c in shared[:count]:
                h_scale(c, z).start()

        gain = TOP / top
        for p in range(PIECES):
            value = hess_own[:, cut(p)]
            for c, step in zip(incoming[:count], steps):
                z_codes(z, z, c, p).wait_recv()
                value = value + z_in[c * PIECES + p].astype(F32) * step
            hess_own[:, cut(p)] = value
            hz[z * PIECES + p] = to_code(value * gain)

            @pl.when(more)
            def _():
                for c in shared[:count]:
                    h_codes(c, z, p).start()

    def expand(c):
        for p in range(PIECES):
            code = hz[c * PIECES + p].astype(jnp.int32)
            upper = lax.shift_right_arithmetic(code, 8)
            split[:vectors, cut(p)] = upper.astype(F32).astype(BF16)
            split[vectors:, cut(p)] = (code & 255).astype(F32).astype(BF16)

    def partial_image(c, columns):
        both = jnp.dot(
            split[...], turned[aligned(c, width), columns], preferred_element_type=F32
        )
        step = get_scale(hz_scale.at[c])
        return (both[:vectors] * 256.0 + both[vectors:]) * step

    def arrive(c):
        h_scale(z, c).wait_recv()
        for p in range(PIECES):
            h_codes(z, c, p).wait_recv()

    def pass_on(dest, chunk):
        h_scale(z, chunk).wait_recv()
        h_scale(dest, chunk, 1).start()
        for p in range(PIECES):
            h_codes(z, chunk, p).wait_recv()
            h_codes(dest, chunk, p, 1).start()

    def passed_sent(dest, chunk):
        h_scale(dest, chunk, 1).wait_send()
        for p in range(PIECES):
            h_codes(dest, chunk, p, 1).wait_send()

    def send_group(p, last):
        for k in range(group):
            q = p * group + k
            if last:

                @pl.when(q != b)
                def _():
                    rs_copy(q, b).start()

            else:
                rs_copy(q, b).start()

    @pl.loop(0, groups)
    def _(s):
        p = lax.rem(b // group + 1 + s, groups)
        part[:, aligned(p, group * span)] = lax.dot_general(
            start_ref[...],
            dense[aligned(p, group * span), :],
            (((1,), (1,)), ((), ())),
            preferred_element_type=F32,
        )
        send_group(p, True)

    def settle_blk():
        @pl.loop(1, n)
        def _(d):
            gb_copy(lax.rem(b + d, n), b, 0).wait_send()

        @pl.loop(1, m)
        def _(d):
            gr_copy(lax.rem(z + d, m), z).wait_send()

    def settle_rows():
        def shared_sent(c):
            h_scale(c, z).wait_send()
            for p in range(PIECES):
                h_codes(c, z, p).wait_send()

        for k in range(takes):
            shared_sent(shared[k])

        if takes < m - 1:

            @pl.when(jnp.logical_not(at_end))
            def _():
                shared_sent(shared[m - 2])

            @pl.when(z == m - 2)
            def _():
                passed_sent(m - 1, 0)

            @pl.when(z == 1)
            def _():
                passed_sent(0, m - 1)

    @pl.loop(0, ITERS)
    def _(it):
        more = it < ITERS - 1
        turn = lax.rem(it, 2)

        @pl.when(it > 0)
        def _():
            settle_blk()
            settle_rows()

        @pl.when(b < owners)
        def _():
            own = part[:, aligned(b, span)]

            def add(d, acc):
                src = lax.rem(b + d, n)
                rs_copy(b, src).wait_recv()
                return acc + rs_buf[src]

            own = sum_over(n, own, add)
            own = jnp.dot(factor[...], own, precision=HIGHEST, preferred_element_type=F32)
            half_own[...] = own.astype(BF16)

            @pl.loop(1, n)
            def _(d):
                ag_copy(lax.rem(b + d, n), b).start()

            half[:, aligned(b, span)] = half_own[...]

        @pl.loop(0, owners)
        def _(q):
            @pl.when(q != b)
            def _():
                ag_copy(b, q).wait_recv()

        held = [send_sum(k) for k in range(sends)]
        hess_own[...] = backward(z)
        for each in held[1:]:
            send_codes(*each)

        if sends < m - 1:

            @pl.when(jnp.logical_not(at_merge))
            def _():
                for k in range(sends, m - 1):
                    each = send_sum(k)
                    if k > 0:
                        send_codes(*each)

            @pl.when(z == 1)
            def _():
                merge(0, m - 1)

            @pl.when(z == m - 2)
            def _():
                merge(1, 0)

        @pl.loop(0, owners)
        def _(q):
            @pl.when(q != b)
            def _():
                rs_copy(q, b).wait_send()

        @pl.when(b < owners)
        def _():
            @pl.loop(1, n)
            def _(d):
                ag_copy(lax.rem(b + d, n), b).wait_send()

        @pl.when(it == 0)
        def _():
            @pl.loop(0, RB)
            def _(r):
                for c in range(CB):
                    turned[c * tile : (c + 1) * tile, aligned(r, tile)] = dense[
                        aligned(r, tile), c * tile : (c + 1) * tile
                    ].T

        @pl.when(at_end)
        def _():
            finish(takes, more)

        if m > 2:

            @pl.when(jnp.logical_not(at_end))
            def _():
                finish(m - 1, more)

        hess = hess_own[...]
        gram = lax.dot_general(
            hess, hess, (((1,), (1,)), ((), ())), precision=HIGHEST, preferred_element_type=F32
        )
        fold = vectors // 2
        gram_own[...] = jnp.concatenate([gram[:fold], gram[fold:]], axis=1)

        @pl.loop(1, n)
        def _(d):
            gb_copy(lax.rem(b + d, n), b, turn).start()

        @pl.when(more)
        def _():
            expand(z)
            part[...] = partial_image(z, slice(None))

        if m > 2:

            @pl.when(jnp.logical_and(more, z == m - 2))
            def _():
                pass_on(m - 1, 0)

            @pl.when(jnp.logical_and(more, z == 1))
            def _():
                pass_on(0, m - 1)

        def add_blk(d, acc):
            src = lax.rem(b + d, n)
            gb_copy(b, src, turn).wait_recv()
            return acc + gram_blk[turn, src]

        gram_line[...] = sum_over(n, gram_own[...], add_blk)

        @pl.loop(1, m)
        def _(d):
            gr_copy(lax.rem(z + d, m), z).start()

        @pl.loop(1, m)
        def _(d):
            there = lax.rem(z + d, m)
            z_scale(there, there, z).wait_send()
            for p in range(PIECES):
                z_codes(there, there, z, p).wait_send()

        @pl.when(more)
        def _():
            arrivals = outgoing[::-1]
            for k, c in enumerate(arrivals):

                @pl.when(jnp.logical_not(merges(c)))
                def _():
                    arrive(c)

                expand(c)
                if k < m - 2:
                    part[...] += partial_image(c, slice(None))
                else:
                    for p in visits:
                        columns = aligned(p, group * span)
                        part[:, columns] += partial_image(c, columns)
                        send_group(p, p is visits[-1])

        def add_line(d, acc):
            src = lax.rem(z + d, m)
            gr_copy(z, src).wait_recv()
            return acc + gram_rows[src]

        packed = sum_over(m, gram_line[...], add_line)
        gram = jnp.concatenate([packed[:, :vectors], packed[:, vectors:]], axis=0) / total
        solved = inverse_factor(gram)
        factor[...] = solved
        out_ref[it] = jnp.dot(
            solved, hess_own[...], precision=HIGHEST, preferred_element_type=F32
        )

    settle_blk()


def local(n, m, sens_tiles, start_basis, row_blocks, col_blocks, live_counts):
    slots, tile = sens_tiles.shape[0], sens_tiles.shape[2]
    vectors, cells = start_basis.shape
    data, width = RB * tile, cells // m
    span = data // min(n, RB)
    piece = width // PIECES
    numbers = jnp.arange(slots, dtype=jnp.int32)
    places = row_blocks[:, 0] * CB + col_blocks[:, 0]
    hit = (places[None, :] == jnp.arange(RB * CB, dtype=jnp.int32)[:, None]) & (
        numbers < live_counts[0, 0]
    )[None, :]
    inv = jnp.min(jnp.where(hit, numbers[None, :], slots), axis=1)
    total = float(cells * n)
    dma = pltpu.SemaphoreType.DMA
    return pl.pallas_call(
        functools.partial(kernel, n, m, total),
        out_shape=jax.ShapeDtypeStruct((ITERS, vectors, width), F32),
        in_specs=[
            pl.BlockSpec(memory_space=pltpu.SMEM),
            pl.BlockSpec(memory_space=pl.ANY),
            pl.BlockSpec(memory_space=pltpu.VMEM),
        ],
        out_specs=pl.BlockSpec(memory_space=pltpu.VMEM),
        scratch_shapes=[
            pltpu.VMEM((slots + 1, tile, tile), BF16),
            pltpu.VMEM((data, cells), BF16),
            pltpu.VMEM((cells, data), BF16),
            pltpu.VMEM((vectors * 2, width), BF16),
            pltpu.VMEM((vectors, vectors), F32),
            pltpu.VMEM((vectors, data), F32),
            pltpu.VMEM((n, vectors, span), F32),
            pltpu.VMEM((vectors, span), BF16),
            pltpu.VMEM((vectors, data), BF16),
            pltpu.VMEM((vectors, width), F32),
            pltpu.VMEM((m * PIECES, vectors, piece), CODE),
            pltpu.VMEM((m, 8, vectors * 2), F32),
            pltpu.VMEM(((m + 2) * PIECES, vectors, piece), CODE),
            pltpu.VMEM((m + 2, 8, vectors * 2), F32),
            pltpu.VMEM((vectors, width), F32),
            pltpu.VMEM((m * PIECES, vectors, piece), CODE),
            pltpu.VMEM((m, 8, vectors * 2), F32),
            pltpu.VMEM((vectors // 2, vectors * 2), F32),
            pltpu.VMEM((m, vectors // 2, vectors * 2), F32),
            pltpu.VMEM((vectors // 2, vectors * 2), F32),
            pltpu.VMEM((2, n, vectors // 2, vectors * 2), F32),
            dma,
            dma((n,)),
            dma((n,)),
            dma((n,)),
            dma((n,)),
            dma((m * PIECES,)),
            dma(((m + 2) * PIECES,)),
            dma((m,)),
            dma((m + 2,)),
            dma((2 * m * PIECES,)),
            dma((m * PIECES,)),
            dma((2 * m,)),
            dma((m,)),
            dma((m,)),
            dma((m,)),
            dma((n,)),
            dma((2, n)),
        ],
        compiler_params=pltpu.CompilerParams(
            collective_id=0, has_side_effects=True, vmem_limit_bytes=56 * 1024 * 1024
        ),
        name="subspace",
    )(inv, sens_tiles, start_basis)


def solution(mesh):
    in_specs = (
        P("blk", "rows", None),
        P(None, "blk"),
        P("blk", "rows"),
        P("blk", "rows"),
        P("blk", "rows"),
    )
    out_specs = P(None, None, ("blk", "rows"))
    return jax.shard_map(
        functools.partial(local, mesh.shape["blk"], mesh.shape["rows"]),
        mesh=mesh,
        in_specs=in_specs,
        out_specs=out_specs,
        check_vma=False,
    )
```

```python
import functools

import jax
import jax.numpy as jnp
from jax import lax
from jax.experimental import pallas as pl
from jax.experimental.pallas import tpu as pltpu
from jax.sharding import PartitionSpec as P

RB = 8
CB = 32
ITERS = 4
MESH = pl.DeviceIdType.MESH
F32 = jnp.float32
BF16 = jnp.bfloat16
HIGHEST = lax.Precision.HIGHEST
CODE = jnp.int16
TOP = 32767.0
PIECES = 2
LOADS = 8


def aligned(index, width):
    return pl.ds(pl.multiple_of(index * width, width), width)


def inverse_factor(gram):
    size = gram.shape[0]
    step = 8
    shape = (step, 2 * size)
    row_id = lax.broadcasted_iota(jnp.int32, (size, size), 0)
    lane_id = lax.broadcasted_iota(jnp.int32, (size, size), 1)
    eye = (row_id == lane_id).astype(F32)
    whole = jnp.concatenate([gram, eye], axis=1)
    blocks = [whole[b * step : (b + 1) * step, :] for b in range(size // step)]
    sub_id = lax.broadcasted_iota(jnp.int32, shape, 0)

    def full(values):
        return jnp.broadcast_to(values, shape)

    outs = []
    for b in range(size // step):
        home, base = blocks[b], b * step
        cols = [full(home[:, base + k : base + k + 1]) for k in range(step)]
        entry = {(i, k): full(cols[k][i : i + 1, :]) for k in range(step) for i in range(k, step)}
        rows = [full(home[k : k + 1, :]) for k in range(step)]
        lower = {
            c: [full(blocks[c][:, base + k : base + k + 1]) for k in range(step)]
            for c in range(b + 1, size // step)
        }
        factor, inverse = {}, []
        for k in range(step):
            inverse.append(1.0 / entry[k, k])
            for i in range(k + 1, step):
                factor[i, k] = entry[i, k] * inverse[k]
            for i in range(k + 1, step):
                for j in range(k + 1, i + 1):
                    entry[i, j] = entry[i, j] - factor[i, k] * entry[j, k]
        for k in range(step):
            for i in range(k + 1, step):
                rows[i] = rows[i] - factor[i, k] * rows[k]
        out = rows[0] * lax.rsqrt(entry[0, 0])
        for k in range(1, step):
            out = jnp.where(sub_id == k, rows[k] * lax.rsqrt(entry[k, k]), out)
        outs.append(out)
        solved = [rows[k] * inverse[k] for k in range(step)]
        for k in reversed(range(step)):
            for i in range(k):
                solved[i] = solved[i] - factor[k, i] * solved[k]
        for c in range(b + 1, size // step):
            terms = [lower[c][k] * solved[k] for k in range(step)]
            while len(terms) > 1:
                terms = [terms[2 * t] + terms[2 * t + 1] for t in range(len(terms) // 2)]
            blocks[c] = blocks[c] - terms[0]
    return jnp.concatenate(outs, axis=0)[:, size:]


def diagonal_of(size):
    row_id = lax.broadcasted_iota(jnp.int32, (size, size), 0)
    return row_id == lax.broadcasted_iota(jnp.int32, (size, size), 1)


def across(column):
    size = column.shape[0]
    return jnp.sum(jnp.where(diagonal_of(size), column, 0.0), axis=0, keepdims=True)


def down(row):
    size = row.shape[1]
    return jnp.sum(jnp.where(diagonal_of(size), row, 0.0), axis=1, keepdims=True)


def peak(values):
    return jnp.maximum(jnp.max(jnp.abs(values), axis=1, keepdims=True), 1e-30)


def put_scale(top, scale_ref):
    size = top.shape[0]
    along = across(top * (1.0 / TOP))
    scale_ref[:, :size] = jnp.broadcast_to(along, (8, size))
    scale_ref[:, size:] = jnp.broadcast_to(along, (8, size))


def get_scale(scale_ref):
    return down(scale_ref[0:1, : scale_ref.shape[1] // 2])


def to_code(values):
    return jnp.round(values).astype(jnp.int32).astype(CODE)


def table(m, z, rows):
    def pick(k):
        value = jnp.int32(0)
        for i in range(m):
            if k < len(rows[i]):
                value = jnp.where(z == i, rows[i][k], value)
        return value

    return [pick(k) for k in range(max(len(row) for row in rows))]


def orders(m):
    outgoing, incoming, shared = [], [], []
    for a in range(m):
        others = sorted((c for c in range(m) if c != a), key=lambda c: -abs(c - a))
        far = {0: m - 1, m - 1: 0}.get(a) if m > 2 else None
        merged = [m - 1] if m > 2 and a == 1 else []
        merged += [0] if m > 2 and a == m - 2 else []
        rest = [c for c in others if c not in merged]
        outgoing.append((rest[::-1] if merged else rest) + merged)
        late = {1: 0, m - 2: m - 1}.get(a)
        nearest = [c for c in reversed(others) if c != far]
        incoming.append(sorted(nearest, key=lambda c: c == late))
        shared.append([c for c in others if c != far])
    return outgoing, incoming, shared


def kernel(
    n,
    m,
    total,
    inv_ref,
    tiles_hbm,
    start_hbm,
    out_hbm,
    tiles,
    start_ref,
    out,
    dense,
    turned,
    split,
    factor,
    part,
    rs_buf,
    half_own,
    half,
    hess_own,
    z_out,
    z_out_scale,
    z_in,
    z_in_scale,
    mid_sum,
    hz,
    hz_scale,
    gram_own,
    gram_rows,
    gram_line,
    gram_blk,
    load_sem,
    start_sem,
    out_sem,
    rs_send,
    rs_recv,
    ag_send,
    ag_recv,
    zc_send,
    zc_recv,
    zs_send,
    zs_recv,
    hc_send,
    hc_recv,
    hs_send,
    hs_recv,
    gr_send,
    gr_recv,
    gb_send,
    gb_recv,
):
    slots = tiles_hbm.shape[0]
    tile = tiles_hbm.shape[1]
    vectors = start_hbm.shape[0]
    data = RB * tile
    cells = start_hbm.shape[1]
    width = cells // m
    owners = min(n, RB)
    span = data // owners
    group = 2 if owners % 2 == 0 else 1
    groups = owners // group
    b = lax.axis_index("blk")
    z = lax.axis_index("rows")
    piece = width // PIECES
    outgoing, incoming, shared = (table(m, z, rows) for rows in orders(m))
    sends = m - 1 if m < 3 else (0 if m == 3 else m - 2)
    takes = m - 1 if m < 3 else m - 2
    near = jnp.where(z == 0, min(1, m - 1), max(m - 2, 0))
    at_end = jnp.logical_or(z == 0, z == m - 1)
    at_merge = jnp.logical_or(z == 1, z == m - 2)

    def far(a, c):
        if m < 3:
            return jnp.bool_(False)
        return jnp.logical_or(
            jnp.logical_and(a == 0, c == m - 1), jnp.logical_and(a == m - 1, c == 0)
        )

    def merges(c):
        if m < 3:
            return jnp.bool_(False)
        return jnp.logical_or(
            jnp.logical_and(z == 1, c == m - 1), jnp.logical_and(z == m - 2, c == 0)
        )

    bulk = slots // LOADS
    loads = [
        pltpu.make_async_copy(
            tiles_hbm.at[pl.ds(k * bulk, bulk)], tiles.at[pl.ds(k * bulk, bulk)], load_sem.at[k]
        )
        for k in range(LOADS)
    ]
    for load in loads:
        load.start()
    first = pltpu.make_async_copy(start_hbm, start_ref, start_sem)
    first.start()

    barrier = pltpu.get_barrier_semaphore()

    @pl.loop(1, n)
    def _(d):
        pl.semaphore_signal(
            barrier, inc=1, device_id={"blk": lax.rem(b + d, n)}, device_id_type=MESH
        )

    @pl.loop(1, m)
    def _(d):
        pl.semaphore_signal(
            barrier, inc=1, device_id={"rows": lax.rem(z + d, m)}, device_id_type=MESH
        )

    tiles[slots] = jnp.zeros((tile, tile), BF16)
    factor[...] = diagonal_of(vectors).astype(F32)
    for load in loads:
        load.wait()

    pl.semaphore_wait(barrier, n - 1 + m - 1)

    here = lax.rem(b // group, groups)
    if groups == 4:
        visits = [3 - here, lax.rem(here + 2, 4), here + 1 - 2 * lax.rem(here, 2), here]
    else:
        visits = [lax.rem(here + 1 + s, groups) for s in range(groups)]

    def sum_over(count, init, term):
        if count > 8:
            return lax.fori_loop(1, count, term, init)
        for d in range(1, count):
            init = term(d, init)
        return init

    def copy(src, dst, send_sem, recv_sem, where):
        return pltpu.make_async_remote_copy(
            src_ref=src,
            dst_ref=dst,
            send_sem=send_sem,
            recv_sem=recv_sem,
            device_id=where,
            device_id_type=MESH,
        )

    def rs_copy(dest, slot):
        return copy(
            part.at[:, aligned(dest, span)],
            rs_buf.at[slot],
            rs_send.at[dest],
            rs_recv.at[slot],
            {"blk": dest},
        )

    def ag_copy(dest, chunk):
        return copy(
            half_own,
            half.at[:, aligned(chunk, span)],
            ag_send.at[dest],
            ag_recv.at[chunk],
            {"blk": dest},
        )

    def z_scale(dest, chunk, slot):
        return copy(
            z_out_scale.at[chunk],
            z_in_scale.at[slot],
            zs_send.at[chunk],
            zs_recv.at[slot],
            {"rows": dest},
        )

    def z_codes(dest, chunk, slot, p):
        k, e = chunk * PIECES + p, slot * PIECES + p
        return copy(z_out.at[k], z_in.at[e], zc_send.at[k], zc_recv.at[e], {"rows": dest})

    def h_scale(dest, slot, passed=0):
        k = passed * m + dest
        return copy(
            hz_scale.at[slot],
            hz_scale.at[slot],
            hs_send.at[k],
            hs_recv.at[slot],
            {"rows": dest},
        )

    def h_codes(dest, slot, p, passed=0):
        k, e = (passed * m + dest) * PIECES + p, slot * PIECES + p
        return copy(hz.at[e], hz.at[e], hc_send.at[k], hc_recv.at[e], {"rows": dest})

    def gr_copy(dest, slot):
        return copy(
            gram_line, gram_rows.at[slot], gr_send.at[dest], gr_recv.at[slot], {"rows": dest}
        )

    def gb_copy(dest, slot, turn):
        return copy(
            gram_own,
            gram_blk.at[turn, slot],
            gb_send.at[dest],
            gb_recv.at[turn, slot],
            {"blk": dest},
        )

    def backward(c):
        return jnp.dot(half[...], dense[:, aligned(c, width)], preferred_element_type=F32)

    def cut(p):
        return slice(p * piece, (p + 1) * piece)

    def send_sum(k):
        c = outgoing[k]
        value = backward(c)
        top = peak(value)
        put_scale(top, z_out_scale.at[c])
        away = far(z, c)
        dest = jnp.where(away, near, c)
        slot = jnp.where(away, jnp.where(z == 0, m, m + 1), z)
        z_scale(dest, c, slot).start()
        gain = TOP / top
        for p in range(PIECES):
            z_out[c * PIECES + p] = to_code(value[:, cut(p)] * gain)
            z_codes(dest, c, slot, p).start()

    def merge(side, c):
        value = backward(c)
        own_top = peak(value)
        slot = m + side
        z_scale(c, c, slot).wait_recv()
        step = get_scale(z_in_scale.at[slot])
        top = step * TOP + own_top
        put_scale(top, z_out_scale.at[c])
        z_scale(c, c, z).start()
        gain = TOP / top
        mid_sum[...] = value * gain
        step = step * gain
        for p in range(PIECES):
            z_codes(c, c, slot, p).wait_recv()
            code = z_in[slot * PIECES + p].astype(F32)
            z_out[c * PIECES + p] = to_code(mid_sum[:, cut(p)] + code * step)
            z_codes(c, c, z, p).start()

    def finish(count, more):
        own_top = peak(hess_own[...])
        steps = []
        for c in incoming[:count]:
            z_scale(z, z, c).wait_recv()
            steps.append(get_scale(z_in_scale.at[c]))
        top = own_top
        for step in steps:
            top = top + step * TOP
        put_scale(top, hz_scale.at[z])

        @pl.when(more)
        def _():
            for c in shared[:count]:
                h_scale(c, z).start()

        gain = TOP / top
        for p in range(PIECES):
            value = hess_own[:, cut(p)]
            for c, step in zip(incoming[:count], steps):
                z_codes(z, z, c, p).wait_recv()
                value = value + z_in[c * PIECES + p].astype(F32) * step
            hess_own[:, cut(p)] = value
            hz[z * PIECES + p] = to_code(value * gain)

            @pl.when(more)
            def _():
                for c in shared[:count]:
                    h_codes(c, z, p).start()

    def expand(c):
        for p in range(PIECES):
            code = hz[c * PIECES + p].astype(jnp.int32)
            upper = lax.shift_right_arithmetic(code, 8)
            split[:vectors, cut(p)] = upper.astype(F32).astype(BF16)
            split[vectors:, cut(p)] = (code & 255).astype(F32).astype(BF16)

    def partial_image(c, columns):
        both = jnp.dot(
            split[...], turned[aligned(c, width), columns], preferred_element_type=F32
        )
        step = get_scale(hz_scale.at[c])
        return (both[:vectors] * 256.0 + both[vectors:]) * step

    def arrive(c):
        h_scale(z, c).wait_recv()
        for p in range(PIECES):
            h_codes(z, c, p).wait_recv()

    def pass_on(dest, chunk):
        h_scale(z, chunk).wait_recv()
        h_scale(dest, chunk, 1).start()
        for p in range(PIECES):
            h_codes(z, chunk, p).wait_recv()
            h_codes(dest, chunk, p, 1).start()

    def passed_sent(dest, chunk):
        h_scale(dest, chunk, 1).wait_send()
        for p in range(PIECES):
            h_codes(dest, chunk, p, 1).wait_send()

    def send_group(p, last):
        for k in range(group):
            q = p * group + k
            if last:

                @pl.when(q != b)
                def _():
                    rs_copy(q, b).start()

            else:
                rs_copy(q, b).start()

    first.wait()

    def place(p):
        @pl.loop(0, RB // groups)
        def _(j):
            r = p * (RB // groups) + j

            @pl.loop(0, CB, unroll=4)
            def _(c):
                dense[aligned(r, tile), aligned(c, tile)] = tiles[inv_ref[r * CB + c]]

    @pl.loop(0, groups)
    def _(s):
        p = lax.rem(b // group + 1 + s, groups)
        place(p)
        part[:, aligned(p, group * span)] = lax.dot_general(
            start_ref[...],
            dense[aligned(p, group * span), :],
            (((1,), (1,)), ((), ())),
            preferred_element_type=F32,
        )
        send_group(p, True)

    def settle_blk():
        @pl.loop(1, n)
        def _(d):
            gb_copy(lax.rem(b + d, n), b, 0).wait_send()

        @pl.loop(1, m)
        def _(d):
            gr_copy(lax.rem(z + d, m), z).wait_send()

    def settle_rows():
        def shared_sent(c):
            h_scale(c, z).wait_send()
            for p in range(PIECES):
                h_codes(c, z, p).wait_send()

        for k in range(takes):
            shared_sent(shared[k])

        if takes < m - 1:

            @pl.when(jnp.logical_not(at_end))
            def _():
                shared_sent(shared[m - 2])

            @pl.when(z == m - 2)
            def _():
                passed_sent(m - 1, 0)

            @pl.when(z == 1)
            def _():
                passed_sent(0, m - 1)

    @pl.loop(0, ITERS)
    def _(it):
        more = it < ITERS - 1
        turn = lax.rem(it, 2)

        @pl.when(it > 0)
        def _():
            settle_blk()
            settle_rows()

        @pl.when(b < owners)
        def _():
            own = part[:, aligned(b, span)]

            def add(d, acc):
                src = lax.rem(b + d, n)
                rs_copy(b, src).wait_recv()
                return acc + rs_buf[src]

            own = sum_over(n, own, add)
            own = jnp.dot(factor[...], own, precision=HIGHEST, preferred_element_type=F32)
            half_own[...] = own.astype(BF16)

            @pl.loop(1, n)
            def _(d):
                ag_copy(lax.rem(b + d, n), b).start()

            half[:, aligned(b, span)] = half_own[...]

        @pl.loop(0, owners)
        def _(q):
            @pl.when(q != b)
            def _():
                ag_copy(b, q).wait_recv()

        for k in range(sends):
            send_sum(k)
        hess_own[...] = backward(z)

        if sends < m - 1:

            @pl.when(jnp.logical_not(at_merge))
            def _():
                for k in range(sends, m - 1):
                    send_sum(k)

            @pl.when(z == 1)
            def _():
                merge(0, m - 1)

            @pl.when(z == m - 2)
            def _():
                merge(1, 0)

        @pl.loop(0, owners)
        def _(q):
            @pl.when(q != b)
            def _():
                rs_copy(q, b).wait_send()

        @pl.when(b < owners)
        def _():
            @pl.loop(1, n)
            def _(d):
                ag_copy(lax.rem(b + d, n), b).wait_send()

        @pl.when(it == 0)
        def _():
            @pl.loop(0, RB)
            def _(r):
                for c in range(CB):
                    turned[c * tile : (c + 1) * tile, aligned(r, tile)] = dense[
                        aligned(r, tile), c * tile : (c + 1) * tile
                    ].T

        @pl.when(at_end)
        def _():
            finish(takes, more)

        if m > 2:

            @pl.when(jnp.logical_not(at_end))
            def _():
                finish(m - 1, more)

        hess = hess_own[...]
        gram = lax.dot_general(
            hess, hess, (((1,), (1,)), ((), ())), precision=HIGHEST, preferred_element_type=F32
        )
        fold = vectors // 2
        gram_own[...] = jnp.concatenate([gram[:fold], gram[fold:]], axis=1)

        @pl.loop(1, n)
        def _(d):
            gb_copy(lax.rem(b + d, n), b, turn).start()

        @pl.when(more)
        def _():
            expand(z)
            part[...] = partial_image(z, slice(None))

        if m > 2:

            @pl.when(jnp.logical_and(more, z == m - 2))
            def _():
                pass_on(m - 1, 0)

            @pl.when(jnp.logical_and(more, z == 1))
            def _():
                pass_on(0, m - 1)

        def add_blk(d, acc):
            src = lax.rem(b + d, n)
            gb_copy(b, src, turn).wait_recv()
            return acc + gram_blk[turn, src]

        gram_line[...] = sum_over(n, gram_own[...], add_blk)

        @pl.loop(1, m)
        def _(d):
            gr_copy(lax.rem(z + d, m), z).start()

        @pl.loop(1, m)
        def _(d):
            there = lax.rem(z + d, m)
            z_scale(there, there, z).wait_send()
            for p in range(PIECES):
                z_codes(there, there, z, p).wait_send()

        @pl.when(more)
        def _():
            arrivals = outgoing[::-1]
            for k, c in enumerate(arrivals):

                @pl.when(jnp.logical_not(merges(c)))
                def _():
                    arrive(c)

                expand(c)
                if k < m - 2:
                    part[...] += partial_image(c, slice(None))
                else:
                    for p in visits:
                        columns = aligned(p, group * span)
                        part[:, columns] += partial_image(c, columns)
                        send_group(p, p is visits[-1])

        def add_line(d, acc):
            src = lax.rem(z + d, m)
            gr_copy(z, src).wait_recv()
            return acc + gram_rows[src]

        packed = sum_over(m, gram_line[...], add_line)
        gram = jnp.concatenate([packed[:, :vectors], packed[:, vectors:]], axis=0) / total
        solved = inverse_factor(gram)
        factor[...] = solved
        out[it] = jnp.dot(solved, hess_own[...], precision=HIGHEST, preferred_element_type=F32)
        pltpu.make_async_copy(out.at[it], out_hbm.at[it], out_sem.at[it]).start()

    settle_blk()

    @pl.loop(0, ITERS)
    def _(it):
        pltpu.make_async_copy(out.at[it], out_hbm.at[it], out_sem.at[it]).wait()


def local(n, m, sens_tiles, start_basis, row_blocks, col_blocks, live_counts):
    slots, tile = sens_tiles.shape[0], sens_tiles.shape[2]
    vectors, cells = start_basis.shape
    data, width = RB * tile, cells // m
    span = data // min(n, RB)
    piece = width // PIECES
    numbers = jnp.arange(slots, dtype=jnp.int32)
    places = row_blocks[:, 0] * CB + col_blocks[:, 0]
    hit = (places[None, :] == jnp.arange(RB * CB, dtype=jnp.int32)[:, None]) & (
        numbers < live_counts[0, 0]
    )[None, :]
    inv = jnp.min(jnp.where(hit, numbers[None, :], slots), axis=1)
    total = float(cells * n)
    dma = pltpu.SemaphoreType.DMA
    return pl.pallas_call(
        functools.partial(kernel, n, m, total),
        out_shape=jax.ShapeDtypeStruct((ITERS, vectors, width), F32),
        in_specs=[
            pl.BlockSpec(memory_space=pltpu.SMEM),
            pl.BlockSpec(memory_space=pl.ANY),
            pl.BlockSpec(memory_space=pl.ANY),
        ],
        out_specs=pl.BlockSpec(memory_space=pl.ANY),
        scratch_shapes=[
            pltpu.VMEM((slots + 1, tile, tile), BF16),
            pltpu.VMEM((vectors, cells), BF16),
            pltpu.VMEM((ITERS, vectors, width), F32),
            pltpu.VMEM((data, cells), BF16),
            pltpu.VMEM((cells, data), BF16),
            pltpu.VMEM((vectors * 2, width), BF16),
            pltpu.VMEM((vectors, vectors), F32),
            pltpu.VMEM((vectors, data), F32),
            pltpu.VMEM((n, vectors, span), F32),
            pltpu.VMEM((vectors, span), BF16),
            pltpu.VMEM((vectors, data), BF16),
            pltpu.VMEM((vectors, width), F32),
            pltpu.VMEM((m * PIECES, vectors, piece), CODE),
            pltpu.VMEM((m, 8, vectors * 2), F32),
            pltpu.VMEM(((m + 2) * PIECES, vectors, piece), CODE),
            pltpu.VMEM((m + 2, 8, vectors * 2), F32),
            pltpu.VMEM((vectors, width), F32),
            pltpu.VMEM((m * PIECES, vectors, piece), CODE),
            pltpu.VMEM((m, 8, vectors * 2), F32),
            pltpu.VMEM((vectors // 2, vectors * 2), F32),
            pltpu.VMEM((m, vectors // 2, vectors * 2), F32),
            pltpu.VMEM((vectors // 2, vectors * 2), F32),
            pltpu.VMEM((2, n, vectors // 2, vectors * 2), F32),
            dma((LOADS,)),
            dma,
            dma((ITERS,)),
            dma((n,)),
            dma((n,)),
            dma((n,)),
            dma((n,)),
            dma((m * PIECES,)),
            dma(((m + 2) * PIECES,)),
            dma((m,)),
            dma((m + 2,)),
            dma((2 * m * PIECES,)),
            dma((m * PIECES,)),
            dma((2 * m,)),
            dma((m,)),
            dma((m,)),
            dma((m,)),
            dma((n,)),
            dma((2, n)),
        ],
        compiler_params=pltpu.CompilerParams(
            collective_id=0, has_side_effects=True, vmem_limit_bytes=56 * 1024 * 1024
        ),
        name="subspace",
    )(inv, sens_tiles, start_basis)


def solution(mesh):
    in_specs = (
        P("blk", "rows", None),
        P(None, "blk"),
        P("blk", "rows"),
        P("blk", "rows"),
        P("blk", "rows"),
    )
    out_specs = P(None, None, ("blk", "rows"))
    return jax.shard_map(
        functools.partial(local, mesh.shape["blk"], mesh.shape["rows"]),
        mesh=mesh,
        in_specs=in_specs,
        out_specs=out_specs,
        check_vma=False,
    )
```

```python
import functools

import jax
import jax.numpy as jnp
from jax import lax
from jax.experimental import pallas as pl
from jax.experimental.pallas import tpu as pltpu
from jax.sharding import PartitionSpec as P

RB = 8
CB = 32
ITERS = 4
MESH = pl.DeviceIdType.MESH
F32 = jnp.float32
BF16 = jnp.bfloat16
HIGHEST = lax.Precision.HIGHEST
CODE = jnp.int16
TOP = 32767.0
PIECES = 2
LOADS = 8


def aligned(index, width):
    return pl.ds(pl.multiple_of(index * width, width), width)


def inverse_factor(gram):
    size = gram.shape[0]
    step = 8
    shape = (step, 2 * size)
    row_id = lax.broadcasted_iota(jnp.int32, (size, size), 0)
    lane_id = lax.broadcasted_iota(jnp.int32, (size, size), 1)
    eye = (row_id == lane_id).astype(F32)
    whole = jnp.concatenate([gram, eye], axis=1)
    blocks = [whole[b * step : (b + 1) * step, :] for b in range(size // step)]
    sub_id = lax.broadcasted_iota(jnp.int32, shape, 0)

    def full(values):
        return jnp.broadcast_to(values, shape)

    outs = []
    for b in range(size // step):
        home, base = blocks[b], b * step
        cols = [full(home[:, base + k : base + k + 1]) for k in range(step)]
        entry = {(i, k): full(cols[k][i : i + 1, :]) for k in range(step) for i in range(k, step)}
        rows = [full(home[k : k + 1, :]) for k in range(step)]
        lower = {
            c: [full(blocks[c][:, base + k : base + k + 1]) for k in range(step)]
            for c in range(b + 1, size // step)
        }
        factor, inverse = {}, []
        for k in range(step):
            inverse.append(1.0 / entry[k, k])
            for i in range(k + 1, step):
                factor[i, k] = entry[i, k] * inverse[k]
            for i in range(k + 1, step):
                for j in range(k + 1, i + 1):
                    entry[i, j] = entry[i, j] - factor[i, k] * entry[j, k]
        for k in range(step):
            for i in range(k + 1, step):
                rows[i] = rows[i] - factor[i, k] * rows[k]
        out = rows[0] * lax.rsqrt(entry[0, 0])
        for k in range(1, step):
            out = jnp.where(sub_id == k, rows[k] * lax.rsqrt(entry[k, k]), out)
        outs.append(out)
        solved = [rows[k] * inverse[k] for k in range(step)]
        for k in reversed(range(step)):
            for i in range(k):
                solved[i] = solved[i] - factor[k, i] * solved[k]
        for c in range(b + 1, size // step):
            terms = [lower[c][k] * solved[k] for k in range(step)]
            while len(terms) > 1:
                terms = [terms[2 * t] + terms[2 * t + 1] for t in range(len(terms) // 2)]
            blocks[c] = blocks[c] - terms[0]
    return jnp.concatenate(outs, axis=0)[:, size:]


def diagonal_of(size):
    row_id = lax.broadcasted_iota(jnp.int32, (size, size), 0)
    return row_id == lax.broadcasted_iota(jnp.int32, (size, size), 1)


def across(column):
    size = column.shape[0]
    return jnp.sum(jnp.where(diagonal_of(size), column, 0.0), axis=0, keepdims=True)


def down(row):
    size = row.shape[1]
    return jnp.sum(jnp.where(diagonal_of(size), row, 0.0), axis=1, keepdims=True)


def peak(values):
    return jnp.maximum(jnp.max(jnp.abs(values), axis=1, keepdims=True), 1e-30)


def put_scale(top, scale_ref):
    size = top.shape[0]
    along = across(top * (1.0 / TOP))
    scale_ref[:, :size] = jnp.broadcast_to(along, (8, size))
    scale_ref[:, size:] = jnp.broadcast_to(along, (8, size))


def get_scale(scale_ref):
    return down(scale_ref[0:1, : scale_ref.shape[1] // 2])


def to_code(values):
    return jnp.round(values).astype(jnp.int32).astype(CODE)


def table(m, z, rows):
    def pick(k):
        value = jnp.int32(0)
        for i in range(m):
            if k < len(rows[i]):
                value = jnp.where(z == i, rows[i][k], value)
        return value

    return [pick(k) for k in range(max(len(row) for row in rows))]


def orders(m):
    outgoing, incoming, shared = [], [], []
    for a in range(m):
        others = sorted((c for c in range(m) if c != a), key=lambda c: -abs(c - a))
        far = {0: m - 1, m - 1: 0}.get(a) if m > 2 else None
        merged = [m - 1] if m > 2 and a == 1 else []
        merged += [0] if m > 2 and a == m - 2 else []
        rest = [c for c in others if c not in merged]
        outgoing.append((rest[::-1] if merged else rest) + merged)
        late = {1: 0, m - 2: m - 1}.get(a)
        nearest = [c for c in reversed(others) if c != far]
        incoming.append(sorted(nearest, key=lambda c: c == late))
        shared.append([c for c in others if c != far])
    return outgoing, incoming, shared


def kernel(
    n,
    m,
    total,
    live_ref,
    row_ref,
    col_ref,
    tiles_hbm,
    start_hbm,
    out_hbm,
    tiles,
    start_ref,
    out,
    dense,
    turned,
    split,
    factor,
    part,
    rs_buf,
    half_own,
    half,
    hess_own,
    z_out,
    z_out_scale,
    z_in,
    z_in_scale,
    mid_sum,
    hz,
    hz_scale,
    gram_own,
    gram_rows,
    gram_line,
    gram_blk,
    inv,
    inv_ref,
    load_sem,
    inv_sem,
    start_sem,
    out_sem,
    rs_send,
    rs_recv,
    ag_send,
    ag_recv,
    zc_send,
    zc_recv,
    zs_send,
    zs_recv,
    hc_send,
    hc_recv,
    hs_send,
    hs_recv,
    gr_send,
    gr_recv,
    gb_send,
    gb_recv,
):
    slots = tiles_hbm.shape[0]
    tile = tiles_hbm.shape[1]
    vectors = start_hbm.shape[0]
    data = RB * tile
    cells = start_hbm.shape[1]
    width = cells // m
    owners = min(n, RB)
    span = data // owners
    group = 2 if owners % 2 == 0 else 1
    groups = owners // group
    b = lax.axis_index("blk")
    z = lax.axis_index("rows")
    piece = width // PIECES
    outgoing, incoming, shared = (table(m, z, rows) for rows in orders(m))
    sends = m - 1 if m < 3 else (0 if m == 3 else m - 2)
    takes = m - 1 if m < 3 else m - 2
    near = jnp.where(z == 0, min(1, m - 1), max(m - 2, 0))
    at_end = jnp.logical_or(z == 0, z == m - 1)
    at_merge = jnp.logical_or(z == 1, z == m - 2)

    def far(a, c):
        if m < 3:
            return jnp.bool_(False)
        return jnp.logical_or(
            jnp.logical_and(a == 0, c == m - 1), jnp.logical_and(a == m - 1, c == 0)
        )

    def merges(c):
        if m < 3:
            return jnp.bool_(False)
        return jnp.logical_or(
            jnp.logical_and(z == 1, c == m - 1), jnp.logical_and(z == m - 2, c == 0)
        )

    bulk = slots // LOADS
    loads = [
        pltpu.make_async_copy(
            tiles_hbm.at[pl.ds(k * bulk, bulk)], tiles.at[pl.ds(k * bulk, bulk)], load_sem.at[k]
        )
        for k in range(LOADS)
    ]
    for load in loads:
        load.start()
    first = pltpu.make_async_copy(start_hbm, start_ref, start_sem)
    first.start()

    number = lax.broadcasted_iota(jnp.int32, (1, slots), 1)
    spot = jnp.where(number < live_ref[0, 0], row_ref[...] * CB + col_ref[...], RB * CB)
    spot = jnp.sum(jnp.where(diagonal_of(slots), spot, 0), axis=1, keepdims=True)
    shape = (slots, RB * CB)
    hit = spot == lax.broadcasted_iota(jnp.int32, shape, 1)
    slot_id = lax.broadcasted_iota(jnp.int32, shape, 0)
    inv[...] = jnp.min(jnp.where(hit, slot_id, slots), axis=0, keepdims=True)
    index = pltpu.make_async_copy(inv, inv_ref, inv_sem)
    index.start()

    barrier = pltpu.get_barrier_semaphore()

    @pl.loop(1, n)
    def _(d):
        pl.semaphore_signal(
            barrier, inc=1, device_id={"blk": lax.rem(b + d, n)}, device_id_type=MESH
        )

    @pl.loop(1, m)
    def _(d):
        pl.semaphore_signal(
            barrier, inc=1, device_id={"rows": lax.rem(z + d, m)}, device_id_type=MESH
        )

    tiles[slots] = jnp.zeros((tile, tile), BF16)
    factor[...] = diagonal_of(vectors).astype(F32)
    index.wait()
    for load in loads:
        load.wait()

    pl.semaphore_wait(barrier, n - 1 + m - 1)

    here = lax.rem(b // group, groups)
    if groups == 4:
        visits = [3 - here, lax.rem(here + 2, 4), here + 1 - 2 * lax.rem(here, 2), here]
    else:
        visits = [lax.rem(here + 1 + s, groups) for s in range(groups)]

    def sum_over(count, init, term):
        if count > 8:
            return lax.fori_loop(1, count, term, init)
        for d in range(1, count):
            init = term(d, init)
        return init

    def copy(src, dst, send_sem, recv_sem, where):
        return pltpu.make_async_remote_copy(
            src_ref=src,
            dst_ref=dst,
            send_sem=send_sem,
            recv_sem=recv_sem,
            device_id=where,
            device_id_type=MESH,
        )

    def rs_copy(dest, slot):
        return copy(
            part.at[:, aligned(dest, span)],
            rs_buf.at[slot],
            rs_send.at[dest],
            rs_recv.at[slot],
            {"blk": dest},
        )

    def ag_copy(dest, chunk):
        return copy(
            half_own,
            half.at[:, aligned(chunk, span)],
            ag_send.at[dest],
            ag_recv.at[chunk],
            {"blk": dest},
        )

    def z_scale(dest, chunk, slot):
        return copy(
            z_out_scale.at[chunk],
            z_in_scale.at[slot],
            zs_send.at[chunk],
            zs_recv.at[slot],
            {"rows": dest},
        )

    def z_codes(dest, chunk, slot, p):
        k, e = chunk * PIECES + p, slot * PIECES + p
        return copy(z_out.at[k], z_in.at[e], zc_send.at[k], zc_recv.at[e], {"rows": dest})

    def h_scale(dest, slot, passed=0):
        k = passed * m + dest
        return copy(
            hz_scale.at[slot],
            hz_scale.at[slot],
            hs_send.at[k],
            hs_recv.at[slot],
            {"rows": dest},
        )

    def h_codes(dest, slot, p, passed=0):
        k, e = (passed * m + dest) * PIECES + p, slot * PIECES + p
        return copy(hz.at[e], hz.at[e], hc_send.at[k], hc_recv.at[e], {"rows": dest})

    def gr_copy(dest, slot):
        return copy(
            gram_line, gram_rows.at[slot], gr_send.at[dest], gr_recv.at[slot], {"rows": dest}
        )

    def gb_copy(dest, slot, turn):
        return copy(
            gram_own,
            gram_blk.at[turn, slot],
            gb_send.at[dest],
            gb_recv.at[turn, slot],
            {"blk": dest},
        )

    def backward(c):
        return jnp.dot(half[...], dense[:, aligned(c, width)], preferred_element_type=F32)

    def cut(p):
        return slice(p * piece, (p + 1) * piece)

    def send_sum(k):
        c = outgoing[k]
        value = backward(c)
        top = peak(value)
        put_scale(top, z_out_scale.at[c])
        away = far(z, c)
        dest = jnp.where(away, near, c)
        slot = jnp.where(away, jnp.where(z == 0, m, m + 1), z)
        z_scale(dest, c, slot).start()
        gain = TOP / top
        for p in range(PIECES):
            z_out[c * PIECES + p] = to_code(value[:, cut(p)] * gain)
            z_codes(dest, c, slot, p).start()

    def merge(side, c):
        value = backward(c)
        own_top = peak(value)
        slot = m + side
        z_scale(c, c, slot).wait_recv()
        step = get_scale(z_in_scale.at[slot])
        top = step * TOP + own_top
        put_scale(top, z_out_scale.at[c])
        z_scale(c, c, z).start()
        gain = TOP / top
        mid_sum[...] = value * gain
        step = step * gain
        for p in range(PIECES):
            z_codes(c, c, slot, p).wait_recv()
            code = z_in[slot * PIECES + p].astype(F32)
            z_out[c * PIECES + p] = to_code(mid_sum[:, cut(p)] + code * step)
            z_codes(c, c, z, p).start()

    def finish(count, more):
        own_top = peak(hess_own[...])
        steps = []
        for c in incoming[:count]:
            z_scale(z, z, c).wait_recv()
            steps.append(get_scale(z_in_scale.at[c]))
        top = own_top
        for step in steps:
            top = top + step * TOP
        put_scale(top, hz_scale.at[z])

        @pl.when(more)
        def _():
            for c in shared[:count]:
                h_scale(c, z).start()

        gain = TOP / top
        for p in range(PIECES):
            value = hess_own[:, cut(p)]
            for c, step in zip(incoming[:count], steps):
                z_codes(z, z, c, p).wait_recv()
                value = value + z_in[c * PIECES + p].astype(F32) * step
            hess_own[:, cut(p)] = value
            hz[z * PIECES + p] = to_code(value * gain)

            @pl.when(more)
            def _():
                for c in shared[:count]:
                    h_codes(c, z, p).start()

    def expand(c):
        for p in range(PIECES):
            code = hz[c * PIECES + p].astype(jnp.int32)
            upper = lax.shift_right_arithmetic(code, 8)
            split[:vectors, cut(p)] = upper.astype(F32).astype(BF16)
            split[vectors:, cut(p)] = (code & 255).astype(F32).astype(BF16)

    def partial_image(c, columns):
        both = jnp.dot(
            split[...], turned[aligned(c, width), columns], preferred_element_type=F32
        )
        step = get_scale(hz_scale.at[c])
        return (both[:vectors] * 256.0 + both[vectors:]) * step

    def arrive(c):
        h_scale(z, c).wait_recv()
        for p in range(PIECES):
            h_codes(z, c, p).wait_recv()

    def pass_on(dest, chunk):
        h_scale(z, chunk).wait_recv()
        h_scale(dest, chunk, 1).start()
        for p in range(PIECES):
            h_codes(z, chunk, p).wait_recv()
            h_codes(dest, chunk, p, 1).start()

    def passed_sent(dest, chunk):
        h_scale(dest, chunk, 1).wait_send()
        for p in range(PIECES):
            h_codes(dest, chunk, p, 1).wait_send()

    def send_group(p, last):
        for k in range(group):
            q = p * group + k
            if last:

                @pl.when(q != b)
                def _():
                    rs_copy(q, b).start()

            else:
                rs_copy(q, b).start()

    first.wait()

    def place(p):
        @pl.loop(0, RB // groups)
        def _(j):
            r = p * (RB // groups) + j

            @pl.loop(0, CB, unroll=4)
            def _(c):
                dense[aligned(r, tile), aligned(c, tile)] = tiles[inv_ref[0, r * CB + c]]

    @pl.loop(0, groups)
    def _(s):
        p = lax.rem(b // group + 1 + s, groups)
        place(p)
        part[:, aligned(p, group * span)] = lax.dot_general(
            start_ref[...],
            dense[aligned(p, group * span), :],
            (((1,), (1,)), ((), ())),
            preferred_element_type=F32,
        )
        send_group(p, True)

    def put_result(k):
        out[k] = jnp.dot(factor[...], hess_own[...], precision=HIGHEST, preferred_element_type=F32)
        pltpu.make_async_copy(out.at[k], out_hbm.at[k], out_sem.at[k]).start()

    def settle_blk():
        @pl.loop(1, n)
        def _(d):
            gb_copy(lax.rem(b + d, n), b, 0).wait_send()

        @pl.loop(1, m)
        def _(d):
            gr_copy(lax.rem(z + d, m), z).wait_send()

    def settle_rows():
        def shared_sent(c):
            h_scale(c, z).wait_send()
            for p in range(PIECES):
                h_codes(c, z, p).wait_send()

        for k in range(takes):
            shared_sent(shared[k])

        if takes < m - 1:

            @pl.when(jnp.logical_not(at_end))
            def _():
                shared_sent(shared[m - 2])

            @pl.when(z == m - 2)
            def _():
                passed_sent(m - 1, 0)

            @pl.when(z == 1)
            def _():
                passed_sent(0, m - 1)

    @pl.loop(0, ITERS)
    def _(it):
        more = it < ITERS - 1
        turn = lax.rem(it, 2)

        @pl.when(b < owners)
        def _():
            own = part[:, aligned(b, span)]

            def add(d, acc):
                src = lax.rem(b + d, n)
                rs_copy(b, src).wait_recv()
                return acc + rs_buf[src]

            own = sum_over(n, own, add)
            own = jnp.dot(factor[...], own, precision=HIGHEST, preferred_element_type=F32)
            half_own[...] = own.astype(BF16)

            @pl.loop(1, n)
            def _(d):
                ag_copy(lax.rem(b + d, n), b).start()

            half[:, aligned(b, span)] = half_own[...]

        @pl.when(it > 0)
        def _():
            put_result(it - 1)
            settle_blk()
            settle_rows()

        @pl.loop(0, owners)
        def _(q):
            @pl.when(q != b)
            def _():
                ag_copy(b, q).wait_recv()

        for k in range(sends):
            send_sum(k)
        hess_own[...] = backward(z)

        if sends < m - 1:

            @pl.when(jnp.logical_not(at_merge))
            def _():
                for k in range(sends, m - 1):
                    send_sum(k)

            @pl.when(z == 1)
            def _():
                merge(0, m - 1)

            @pl.when(z == m - 2)
            def _():
                merge(1, 0)

        @pl.loop(0, owners)
        def _(q):
            @pl.when(q != b)
            def _():
                rs_copy(q, b).wait_send()

        @pl.when(b < owners)
        def _():
            @pl.loop(1, n)
            def _(d):
                ag_copy(lax.rem(b + d, n), b).wait_send()

        @pl.when(it == 0)
        def _():
            @pl.loop(0, RB)
            def _(r):
                for c in range(CB):
                    turned[c * tile : (c + 1) * tile, aligned(r, tile)] = dense[
                        aligned(r, tile), c * tile : (c + 1) * tile
                    ].T

        @pl.when(at_end)
        def _():
            finish(takes, more)

        if m > 2:

            @pl.when(jnp.logical_not(at_end))
            def _():
                finish(m - 1, more)

        hess = hess_own[...]
        gram = lax.dot_general(
            hess, hess, (((1,), (1,)), ((), ())), precision=HIGHEST, preferred_element_type=F32
        )
        fold = vectors // 2
        gram_own[...] = jnp.concatenate([gram[:fold], gram[fold:]], axis=1)

        @pl.loop(1, n)
        def _(d):
            gb_copy(lax.rem(b + d, n), b, turn).start()

        @pl.when(more)
        def _():
            expand(z)
            part[...] = partial_image(z, slice(None))

        if m > 2:

            @pl.when(jnp.logical_and(more, z == m - 2))
            def _():
                pass_on(m - 1, 0)

            @pl.when(jnp.logical_and(more, z == 1))
            def _():
                pass_on(0, m - 1)

        def add_blk(d, acc):
            src = lax.rem(b + d, n)
            gb_copy(b, src, turn).wait_recv()
            return acc + gram_blk[turn, src]

        gram_line[...] = sum_over(n, gram_own[...], add_blk)

        @pl.loop(1, m)
        def _(d):
            gr_copy(lax.rem(z + d, m), z).start()

        @pl.loop(1, m)
        def _(d):
            there = lax.rem(z + d, m)
            z_scale(there, there, z).wait_send()
            for p in range(PIECES):
                z_codes(there, there, z, p).wait_send()

        @pl.when(more)
        def _():
            arrivals = outgoing[::-1]
            for k, c in enumerate(arrivals):

                @pl.when(jnp.logical_not(merges(c)))
                def _():
                    arrive(c)

                expand(c)
                if k < m - 2:
                    part[...] += partial_image(c, slice(None))
                else:
                    for p in visits:
                        columns = aligned(p, group * span)
                        part[:, columns] += partial_image(c, columns)
                        send_group(p, p is visits[-1])

        def add_line(d, acc):
            src = lax.rem(z + d, m)
            gr_copy(z, src).wait_recv()
            return acc + gram_rows[src]

        packed = sum_over(m, gram_line[...], add_line)
        gram = jnp.concatenate([packed[:, :vectors], packed[:, vectors:]], axis=0) / total
        factor[...] = inverse_factor(gram)

    put_result(ITERS - 1)
    settle_blk()

    @pl.loop(0, ITERS)
    def _(it):
        pltpu.make_async_copy(out.at[it], out_hbm.at[it], out_sem.at[it]).wait()


def local(n, m, sens_tiles, start_basis, row_blocks, col_blocks, live_counts):
    slots, tile = sens_tiles.shape[0], sens_tiles.shape[2]
    vectors, cells = start_basis.shape
    data, width = RB * tile, cells // m
    span = data // min(n, RB)
    piece = width // PIECES
    total = float(cells * n)
    dma = pltpu.SemaphoreType.DMA
    return pl.pallas_call(
        functools.partial(kernel, n, m, total),
        out_shape=jax.ShapeDtypeStruct((ITERS, vectors, width), F32),
        in_specs=[
            pl.BlockSpec(memory_space=pltpu.SMEM),
            pl.BlockSpec(memory_space=pltpu.VMEM),
            pl.BlockSpec(memory_space=pltpu.VMEM),
            pl.BlockSpec(memory_space=pl.ANY),
            pl.BlockSpec(memory_space=pl.ANY),
        ],
        out_specs=pl.BlockSpec(memory_space=pl.ANY),
        scratch_shapes=[
            pltpu.VMEM((slots + 1, tile, tile), BF16),
            pltpu.VMEM((vectors, cells), BF16),
            pltpu.VMEM((ITERS, vectors, width), F32),
            pltpu.VMEM((data, cells), BF16),
            pltpu.VMEM((cells, data), BF16),
            pltpu.VMEM((vectors * 2, width), BF16),
            pltpu.VMEM((vectors, vectors), F32),
            pltpu.VMEM((vectors, data), F32),
            pltpu.VMEM((n, vectors, span), F32),
            pltpu.VMEM((vectors, span), BF16),
            pltpu.VMEM((vectors, data), BF16),
            pltpu.VMEM((vectors, width), F32),
            pltpu.VMEM((m * PIECES, vectors, piece), CODE),
            pltpu.VMEM((m, 8, vectors * 2), F32),
            pltpu.VMEM(((m + 2) * PIECES, vectors, piece), CODE),
            pltpu.VMEM((m + 2, 8, vectors * 2), F32),
            pltpu.VMEM((vectors, width), F32),
            pltpu.VMEM((m * PIECES, vectors, piece), CODE),
            pltpu.VMEM((m, 8, vectors * 2), F32),
            pltpu.VMEM((vectors // 2, vectors * 2), F32),
            pltpu.VMEM((m, vectors // 2, vectors * 2), F32),
            pltpu.VMEM((vectors // 2, vectors * 2), F32),
            pltpu.VMEM((2, n, vectors // 2, vectors * 2), F32),
            pltpu.VMEM((1, RB * CB), jnp.int32),
            pltpu.SMEM((1, RB * CB), jnp.int32),
            dma((LOADS,)),
            dma,
            dma,
            dma((ITERS,)),
            dma((n,)),
            dma((n,)),
            dma((n,)),
            dma((n,)),
            dma((m * PIECES,)),
            dma(((m + 2) * PIECES,)),
            dma((m,)),
            dma((m + 2,)),
            dma((2 * m * PIECES,)),
            dma((m * PIECES,)),
            dma((2 * m,)),
            dma((m,)),
            dma((m,)),
            dma((m,)),
            dma((n,)),
            dma((2, n)),
        ],
        compiler_params=pltpu.CompilerParams(
            collective_id=0, has_side_effects=True, vmem_limit_bytes=56 * 1024 * 1024
        ),
        name="subspace",
    )(
        live_counts,
        row_blocks.reshape(1, slots),
        col_blocks.reshape(1, slots),
        sens_tiles,
        start_basis,
    )


def solution(mesh):
    in_specs = (
        P("blk", "rows", None),
        P(None, "blk"),
        P("blk", "rows"),
        P("blk", "rows"),
        P("blk", "rows"),
    )
    out_specs = P(None, None, ("blk", "rows"))
    return jax.shard_map(
        functools.partial(local, mesh.shape["blk"], mesh.shape["rows"]),
        mesh=mesh,
        in_specs=in_specs,
        out_specs=out_specs,
        check_vma=False,
    )
```

```python
import functools

import jax
import jax.numpy as jnp
from jax import lax
from jax.experimental import pallas as pl
from jax.experimental.pallas import tpu as pltpu
from jax.sharding import PartitionSpec as P

RB = 8
CB = 32
ITERS = 4
MESH = pl.DeviceIdType.MESH
F32 = jnp.float32
BF16 = jnp.bfloat16
HIGHEST = lax.Precision.HIGHEST
CODE = jnp.int16
TOP = 32767.0
PIECES = 2
LOADS = 8


def aligned(index, width):
    return pl.ds(pl.multiple_of(index * width, width), width)


def inverse_factor(gram):
    size = gram.shape[0]
    step = 8
    shape = (step, 2 * size)
    row_id = lax.broadcasted_iota(jnp.int32, (size, size), 0)
    lane_id = lax.broadcasted_iota(jnp.int32, (size, size), 1)
    eye = (row_id == lane_id).astype(F32)
    whole = jnp.concatenate([gram, eye], axis=1)
    blocks = [whole[b * step : (b + 1) * step, :] for b in range(size // step)]
    sub_id = lax.broadcasted_iota(jnp.int32, shape, 0)

    def full(values):
        return jnp.broadcast_to(values, shape)

    outs = []
    for b in range(size // step):
        home, base = blocks[b], b * step
        cols = [full(home[:, base + k : base + k + 1]) for k in range(step)]
        entry = {(i, k): full(cols[k][i : i + 1, :]) for k in range(step) for i in range(k, step)}
        rows = [full(home[k : k + 1, :]) for k in range(step)]
        lower = {
            c: [full(blocks[c][:, base + k : base + k + 1]) for k in range(step)]
            for c in range(b + 1, size // step)
        }
        factor, inverse = {}, []
        for k in range(step):
            inverse.append(1.0 / entry[k, k])
            for i in range(k + 1, step):
                factor[i, k] = entry[i, k] * inverse[k]
            for i in range(k + 1, step):
                for j in range(k + 1, i + 1):
                    entry[i, j] = entry[i, j] - factor[i, k] * entry[j, k]
        for k in range(step):
            for i in range(k + 1, step):
                rows[i] = rows[i] - factor[i, k] * rows[k]
        out = rows[0] * lax.rsqrt(entry[0, 0])
        for k in range(1, step):
            out = jnp.where(sub_id == k, rows[k] * lax.rsqrt(entry[k, k]), out)
        outs.append(out)
        solved = [rows[k] * inverse[k] for k in range(step)]
        for k in reversed(range(step)):
            for i in range(k):
                solved[i] = solved[i] - factor[k, i] * solved[k]
        for c in range(b + 1, size // step):
            terms = [lower[c][k] * solved[k] for k in range(step)]
            while len(terms) > 1:
                terms = [terms[2 * t] + terms[2 * t + 1] for t in range(len(terms) // 2)]
            blocks[c] = blocks[c] - terms[0]
    return jnp.concatenate(outs, axis=0)[:, size:]


def diagonal_of(size):
    row_id = lax.broadcasted_iota(jnp.int32, (size, size), 0)
    return row_id == lax.broadcasted_iota(jnp.int32, (size, size), 1)


def across(column):
    size = column.shape[0]
    return jnp.sum(jnp.where(diagonal_of(size), column, 0.0), axis=0, keepdims=True)


def down(row):
    size = row.shape[1]
    return jnp.sum(jnp.where(diagonal_of(size), row, 0.0), axis=1, keepdims=True)


def peak(values):
    return jnp.maximum(jnp.max(jnp.abs(values), axis=1, keepdims=True), 1e-30)


def put_scale(top, scale_ref):
    size = top.shape[0]
    along = across(top * (1.0 / TOP))
    scale_ref[:, :size] = jnp.broadcast_to(along, (8, size))
    scale_ref[:, size:] = jnp.broadcast_to(along, (8, size))


def get_scale(scale_ref):
    return down(scale_ref[0:1, : scale_ref.shape[1] // 2])


def to_code(values):
    return jnp.round(values).astype(jnp.int32).astype(CODE)


def table(m, z, rows):
    def pick(k):
        value = jnp.int32(0)
        for i in range(m):
            if k < len(rows[i]):
                value = jnp.where(z == i, rows[i][k], value)
        return value

    return [pick(k) for k in range(max(len(row) for row in rows))]


def orders(m):
    outgoing, incoming, shared = [], [], []
    for a in range(m):
        others = sorted((c for c in range(m) if c != a), key=lambda c: -abs(c - a))
        far = {0: m - 1, m - 1: 0}.get(a) if m > 2 else None
        merged = [m - 1] if m > 2 and a == 1 else []
        merged += [0] if m > 2 and a == m - 2 else []
        rest = [c for c in others if c not in merged]
        outgoing.append((rest[::-1] if merged else rest) + merged)
        late = {1: 0, m - 2: m - 1}.get(a)
        nearest = [c for c in reversed(others) if c != far]
        incoming.append(sorted(nearest, key=lambda c: c == late))
        shared.append([c for c in others if c != far])
    return outgoing, incoming, shared


def kernel(
    n,
    m,
    total,
    live_ref,
    row_ref,
    col_ref,
    tiles_hbm,
    start_hbm,
    out_hbm,
    tiles,
    start_ref,
    out,
    dense,
    turned,
    split,
    factor,
    part,
    rs_buf,
    half_own,
    half,
    hess_own,
    z_out,
    z_out_scale,
    z_in,
    z_in_scale,
    mid_sum,
    hz,
    hz_scale,
    gram_own,
    gram_rows,
    gram_line,
    gram_blk,
    inv,
    inv_ref,
    load_sem,
    inv_sem,
    start_sem,
    out_sem,
    rs_send,
    rs_recv,
    ag_send,
    ag_recv,
    zc_send,
    zc_recv,
    zs_send,
    zs_recv,
    hc_send,
    hc_recv,
    hs_send,
    hs_recv,
    gr_send,
    gr_recv,
    gb_send,
    gb_recv,
):
    slots = tiles_hbm.shape[0]
    tile = tiles_hbm.shape[1]
    vectors = start_hbm.shape[0]
    data = RB * tile
    cells = start_hbm.shape[1]
    width = cells // m
    owners = min(n, RB)
    span = data // owners
    group = 2 if owners % 2 == 0 else 1
    groups = owners // group
    b = lax.axis_index("blk")
    z = lax.axis_index("rows")
    piece = width // PIECES
    outgoing, incoming, shared = (table(m, z, rows) for rows in orders(m))
    sends = m - 1 if m < 3 else (0 if m == 3 else m - 2)
    takes = m - 1 if m < 3 else m - 2
    near = jnp.where(z == 0, min(1, m - 1), max(m - 2, 0))
    at_end = jnp.logical_or(z == 0, z == m - 1)
    at_merge = jnp.logical_or(z == 1, z == m - 2)

    def far(a, c):
        if m < 3:
            return jnp.bool_(False)
        return jnp.logical_or(
            jnp.logical_and(a == 0, c == m - 1), jnp.logical_and(a == m - 1, c == 0)
        )

    def merges(c):
        if m < 3:
            return jnp.bool_(False)
        return jnp.logical_or(
            jnp.logical_and(z == 1, c == m - 1), jnp.logical_and(z == m - 2, c == 0)
        )

    bulk = slots // LOADS
    loads = [
        pltpu.make_async_copy(
            tiles_hbm.at[pl.ds(k * bulk, bulk)], tiles.at[pl.ds(k * bulk, bulk)], load_sem.at[k]
        )
        for k in range(LOADS)
    ]
    for load in loads:
        load.start()
    first = pltpu.make_async_copy(start_hbm, start_ref, start_sem)
    first.start()

    number = lax.broadcasted_iota(jnp.int32, (1, slots), 1)
    spot = jnp.where(number < live_ref[0, 0], row_ref[...] * CB + col_ref[...], RB * CB)
    spot = jnp.sum(jnp.where(diagonal_of(slots), spot, 0), axis=1, keepdims=True)
    shape = (slots, RB * CB)
    hit = spot == lax.broadcasted_iota(jnp.int32, shape, 1)
    slot_id = lax.broadcasted_iota(jnp.int32, shape, 0)
    inv[...] = jnp.min(jnp.where(hit, slot_id, slots), axis=0, keepdims=True)
    index = pltpu.make_async_copy(inv, inv_ref, inv_sem)
    index.start()

    barrier = pltpu.get_barrier_semaphore()

    @pl.loop(1, n)
    def _(d):
        pl.semaphore_signal(
            barrier, inc=1, device_id={"blk": lax.rem(b + d, n)}, device_id_type=MESH
        )

    @pl.loop(1, m)
    def _(d):
        pl.semaphore_signal(
            barrier, inc=1, device_id={"rows": lax.rem(z + d, m)}, device_id_type=MESH
        )

    tiles[slots] = jnp.zeros((tile, tile), BF16)
    factor[...] = diagonal_of(vectors).astype(F32)
    index.wait()
    for load in loads:
        load.wait()

    pl.semaphore_wait(barrier, n - 1 + m - 1)

    here = lax.rem(b // group, groups)
    if groups == 4:
        visits = [3 - here, lax.rem(here + 2, 4), here + 1 - 2 * lax.rem(here, 2), here]
    else:
        visits = [lax.rem(here + 1 + s, groups) for s in range(groups)]

    def sum_over(count, init, term):
        if count > 8:
            return lax.fori_loop(1, count, term, init)
        for d in range(1, count):
            init = term(d, init)
        return init

    def copy(src, dst, send_sem, recv_sem, where):
        return pltpu.make_async_remote_copy(
            src_ref=src,
            dst_ref=dst,
            send_sem=send_sem,
            recv_sem=recv_sem,
            device_id=where,
            device_id_type=MESH,
        )

    def rs_copy(dest, slot):
        return copy(
            part.at[:, aligned(dest, span)],
            rs_buf.at[slot],
            rs_send.at[dest],
            rs_recv.at[slot],
            {"blk": dest},
        )

    def ag_copy(dest, chunk):
        return copy(
            half_own,
            half.at[:, aligned(chunk, span)],
            ag_send.at[dest],
            ag_recv.at[chunk],
            {"blk": dest},
        )

    def z_scale(dest, chunk, slot):
        return copy(
            z_out_scale.at[chunk],
            z_in_scale.at[slot],
            zs_send.at[chunk],
            zs_recv.at[slot],
            {"rows": dest},
        )

    def z_codes(dest, chunk, slot, p):
        k, e = chunk * PIECES + p, slot * PIECES + p
        return copy(z_out.at[k], z_in.at[e], zc_send.at[k], zc_recv.at[e], {"rows": dest})

    def h_scale(dest, slot, passed=0):
        k = passed * m + dest
        return copy(
            hz_scale.at[slot],
            hz_scale.at[slot],
            hs_send.at[k],
            hs_recv.at[slot],
            {"rows": dest},
        )

    def h_codes(dest, slot, p, passed=0):
        k, e = (passed * m + dest) * PIECES + p, slot * PIECES + p
        return copy(hz.at[e], hz.at[e], hc_send.at[k], hc_recv.at[e], {"rows": dest})

    def gr_copy(dest, slot):
        return copy(
            gram_line, gram_rows.at[slot], gr_send.at[dest], gr_recv.at[slot], {"rows": dest}
        )

    def gb_copy(dest, slot, turn):
        return copy(
            gram_own,
            gram_blk.at[turn, slot],
            gb_send.at[dest],
            gb_recv.at[turn, slot],
            {"blk": dest},
        )

    def backward(c):
        return jnp.dot(half[...], dense[:, aligned(c, width)], preferred_element_type=F32)

    def cut(p):
        return slice(p * piece, (p + 1) * piece)

    def send_sum(k):
        c = outgoing[k]
        value = backward(c)
        top = peak(value)
        put_scale(top, z_out_scale.at[c])
        away = far(z, c)
        dest = jnp.where(away, near, c)
        slot = jnp.where(away, jnp.where(z == 0, m, m + 1), z)
        z_scale(dest, c, slot).start()
        gain = TOP / top
        for p in range(PIECES):
            z_out[c * PIECES + p] = to_code(value[:, cut(p)] * gain)
            z_codes(dest, c, slot, p).start()

    def merge(side, c):
        value = backward(c)
        own_top = peak(value)
        slot = m + side
        z_scale(c, c, slot).wait_recv()
        step = get_scale(z_in_scale.at[slot])
        top = step * TOP + own_top
        put_scale(top, z_out_scale.at[c])
        z_scale(c, c, z).start()
        gain = TOP / top
        mid_sum[...] = value * gain
        step = step * gain
        for p in range(PIECES):
            z_codes(c, c, slot, p).wait_recv()
            code = z_in[slot * PIECES + p].astype(F32)
            z_out[c * PIECES + p] = to_code(mid_sum[:, cut(p)] + code * step)
            z_codes(c, c, z, p).start()

    def finish(count, more):
        own_top = peak(hess_own[...])
        steps = []
        for c in incoming[:count]:
            z_scale(z, z, c).wait_recv()
            steps.append(get_scale(z_in_scale.at[c]))
        top = own_top
        for step in steps:
            top = top + step * TOP
        put_scale(top, hz_scale.at[z])

        @pl.when(more)
        def _():
            for c in shared[:count]:
                h_scale(c, z).start()

        gain = TOP / top
        for p in range(PIECES):
            value = hess_own[:, cut(p)]
            for c, step in zip(incoming[:count], steps):
                z_codes(z, z, c, p).wait_recv()
                value = value + z_in[c * PIECES + p].astype(F32) * step
            hess_own[:, cut(p)] = value
            hz[z * PIECES + p] = to_code(value * gain)

            @pl.when(more)
            def _():
                for c in shared[:count]:
                    h_codes(c, z, p).start()

    def expand(c):
        for p in range(PIECES):
            code = hz[c * PIECES + p].astype(jnp.int32)
            upper = lax.shift_right_arithmetic(code, 8)
            split[:vectors, cut(p)] = upper.astype(F32).astype(BF16)
            split[vectors:, cut(p)] = (code & 255).astype(F32).astype(BF16)

    def partial_image(c, columns):
        both = jnp.dot(
            split[...], turned[aligned(c, width), columns], preferred_element_type=F32
        )
        step = get_scale(hz_scale.at[c])
        return (both[:vectors] * 256.0 + both[vectors:]) * step

    def arrive(c):
        h_scale(z, c).wait_recv()
        for p in range(PIECES):
            h_codes(z, c, p).wait_recv()

    def pass_on(dest, chunk):
        h_scale(z, chunk).wait_recv()
        h_scale(dest, chunk, 1).start()
        for p in range(PIECES):
            h_codes(z, chunk, p).wait_recv()
            h_codes(dest, chunk, p, 1).start()

    def passed_sent(dest, chunk):
        h_scale(dest, chunk, 1).wait_send()
        for p in range(PIECES):
            h_codes(dest, chunk, p, 1).wait_send()

    def send_group(p, last):
        for k in range(group):
            q = p * group + k
            if last:

                @pl.when(q != b)
                def _():
                    rs_copy(q, b).start()

            else:
                rs_copy(q, b).start()

    first.wait()

    def place(p):
        @pl.loop(0, RB // groups)
        def _(j):
            r = p * (RB // groups) + j

            @pl.loop(0, CB, unroll=4)
            def _(c):
                dense[aligned(r, tile), aligned(c, tile)] = tiles[inv_ref[0, r * CB + c]]

    @pl.loop(0, groups)
    def _(s):
        p = lax.rem(b // group + 1 + s, groups)
        place(p)
        part[:, aligned(p, group * span)] = lax.dot_general(
            start_ref[...],
            dense[aligned(p, group * span), :],
            (((1,), (1,)), ((), ())),
            preferred_element_type=F32,
        )
        send_group(p, True)

    def put_result(k):
        out[k] = jnp.dot(factor[...], hess_own[...], precision=HIGHEST, preferred_element_type=F32)
        pltpu.make_async_copy(out.at[k], out_hbm.at[k], out_sem.at[k]).start()

    def settle_blk():
        @pl.loop(1, n)
        def _(d):
            gb_copy(lax.rem(b + d, n), b, 0).wait_send()

        @pl.loop(1, m)
        def _(d):
            gr_copy(lax.rem(z + d, m), z).wait_send()

    def settle_rows():
        def shared_sent(c):
            h_scale(c, z).wait_send()
            for p in range(PIECES):
                h_codes(c, z, p).wait_send()

        for k in range(takes):
            shared_sent(shared[k])

        if takes < m - 1:

            @pl.when(jnp.logical_not(at_end))
            def _():
                shared_sent(shared[m - 2])

            @pl.when(z == m - 2)
            def _():
                passed_sent(m - 1, 0)

            @pl.when(z == 1)
            def _():
                passed_sent(0, m - 1)

    @pl.loop(0, ITERS)
    def _(it):
        more = it < ITERS - 1
        turn = lax.rem(it, 2)

        @pl.when(b < owners)
        def _():
            own = part[:, aligned(b, span)]

            def add(d, acc):
                src = lax.rem(b + d, n)
                rs_copy(b, src).wait_recv()
                return acc + rs_buf[src]

            own = sum_over(n, own, add)
            own = jnp.dot(factor[...], own, precision=HIGHEST, preferred_element_type=F32)
            half_own[...] = own.astype(BF16)

            if n == owners:
                for p in visits:
                    for k in range(group):
                        q = p * group + k
                        if p is visits[-1]:

                            @pl.when(q != b)
                            def _():
                                ag_copy(q, b).start()

                        else:
                            ag_copy(q, b).start()
            else:

                @pl.loop(1, n)
                def _(d):
                    ag_copy(lax.rem(b + d, n), b).start()

            half[:, aligned(b, span)] = half_own[...]

        @pl.when(it > 0)
        def _():
            put_result(it - 1)
            settle_blk()
            settle_rows()

        for d in range(1, owners) if n == owners else ():
            ag_copy(b, lax.rem(b + d, n)).wait_recv()

        @pl.loop(0, owners if n > owners else 0)
        def _(q):
            @pl.when(q != b)
            def _():
                ag_copy(b, q).wait_recv()

        for k in range(sends):
            send_sum(k)
        hess_own[...] = backward(z)

        if sends < m - 1:

            @pl.when(jnp.logical_not(at_merge))
            def _():
                for k in range(sends, m - 1):
                    send_sum(k)

            @pl.when(z == 1)
            def _():
                merge(0, m - 1)

            @pl.when(z == m - 2)
            def _():
                merge(1, 0)

        @pl.loop(0, owners)
        def _(q):
            @pl.when(q != b)
            def _():
                rs_copy(q, b).wait_send()

        @pl.when(b < owners)
        def _():
            @pl.loop(1, n)
            def _(d):
                ag_copy(lax.rem(b + d, n), b).wait_send()

        @pl.when(it == 0)
        def _():
            @pl.loop(0, RB)
            def _(r):
                for c in range(CB):
                    turned[c * tile : (c + 1) * tile, aligned(r, tile)] = dense[
                        aligned(r, tile), c * tile : (c + 1) * tile
                    ].T

        @pl.when(at_end)
        def _():
            finish(takes, more)

        if m > 2:

            @pl.when(jnp.logical_not(at_end))
            def _():
                finish(m - 1, more)

        hess = hess_own[...]
        gram = lax.dot_general(
            hess, hess, (((1,), (1,)), ((), ())), precision=HIGHEST, preferred_element_type=F32
        )
        fold = vectors // 2
        gram_own[...] = jnp.concatenate([gram[:fold], gram[fold:]], axis=1)

        @pl.loop(1, n)
        def _(d):
            gb_copy(lax.rem(b + d, n), b, turn).start()

        @pl.when(more)
        def _():
            expand(z)
            part[...] = partial_image(z, slice(None))

        if m > 2:

            @pl.when(jnp.logical_and(more, z == m - 2))
            def _():
                pass_on(m - 1, 0)

            @pl.when(jnp.logical_and(more, z == 1))
            def _():
                pass_on(0, m - 1)

        def add_blk(d, acc):
            src = lax.rem(b + d, n)
            gb_copy(b, src, turn).wait_recv()
            return acc + gram_blk[turn, src]

        gram_line[...] = sum_over(n, gram_own[...], add_blk)

        @pl.loop(1, m)
        def _(d):
            gr_copy(lax.rem(z + d, m), z).start()

        @pl.loop(1, m)
        def _(d):
            there = lax.rem(z + d, m)
            z_scale(there, there, z).wait_send()
            for p in range(PIECES):
                z_codes(there, there, z, p).wait_send()

        @pl.when(more)
        def _():
            arrivals = outgoing[::-1]
            for k, c in enumerate(arrivals):

                @pl.when(jnp.logical_not(merges(c)))
                def _():
                    arrive(c)

                expand(c)
                if k < m - 2:
                    part[...] += partial_image(c, slice(None))
                else:
                    for p in visits:
                        columns = aligned(p, group * span)
                        part[:, columns] += partial_image(c, columns)
                        send_group(p, p is visits[-1])

        def add_line(d, acc):
            src = lax.rem(z + d, m)
            gr_copy(z, src).wait_recv()
            return acc + gram_rows[src]

        packed = sum_over(m, gram_line[...], add_line)
        gram = jnp.concatenate([packed[:, :vectors], packed[:, vectors:]], axis=0) / total
        factor[...] = inverse_factor(gram)

    put_result(ITERS - 1)
    settle_blk()

    @pl.loop(0, ITERS)
    def _(it):
        pltpu.make_async_copy(out.at[it], out_hbm.at[it], out_sem.at[it]).wait()


def local(n, m, sens_tiles, start_basis, row_blocks, col_blocks, live_counts):
    slots, tile = sens_tiles.shape[0], sens_tiles.shape[2]
    vectors, cells = start_basis.shape
    data, width = RB * tile, cells // m
    span = data // min(n, RB)
    piece = width // PIECES
    total = float(cells * n)
    dma = pltpu.SemaphoreType.DMA
    return pl.pallas_call(
        functools.partial(kernel, n, m, total),
        out_shape=jax.ShapeDtypeStruct((ITERS, vectors, width), F32),
        in_specs=[
            pl.BlockSpec(memory_space=pltpu.SMEM),
            pl.BlockSpec(memory_space=pltpu.VMEM),
            pl.BlockSpec(memory_space=pltpu.VMEM),
            pl.BlockSpec(memory_space=pl.ANY),
            pl.BlockSpec(memory_space=pl.ANY),
        ],
        out_specs=pl.BlockSpec(memory_space=pl.ANY),
        scratch_shapes=[
            pltpu.VMEM((slots + 1, tile, tile), BF16),
            pltpu.VMEM((vectors, cells), BF16),
            pltpu.VMEM((ITERS, vectors, width), F32),
            pltpu.VMEM((data, cells), BF16),
            pltpu.VMEM((cells, data), BF16),
            pltpu.VMEM((vectors * 2, width), BF16),
            pltpu.VMEM((vectors, vectors), F32),
            pltpu.VMEM((vectors, data), F32),
            pltpu.VMEM((n, vectors, span), F32),
            pltpu.VMEM((vectors, span), BF16),
            pltpu.VMEM((vectors, data), BF16),
            pltpu.VMEM((vectors, width), F32),
            pltpu.VMEM((m * PIECES, vectors, piece), CODE),
            pltpu.VMEM((m, 8, vectors * 2), F32),
            pltpu.VMEM(((m + 2) * PIECES, vectors, piece), CODE),
            pltpu.VMEM((m + 2, 8, vectors * 2), F32),
            pltpu.VMEM((vectors, width), F32),
            pltpu.VMEM((m * PIECES, vectors, piece), CODE),
            pltpu.VMEM((m, 8, vectors * 2), F32),
            pltpu.VMEM((vectors // 2, vectors * 2), F32),
            pltpu.VMEM((m, vectors // 2, vectors * 2), F32),
            pltpu.VMEM((vectors // 2, vectors * 2), F32),
            pltpu.VMEM((2, n, vectors // 2, vectors * 2), F32),
            pltpu.VMEM((1, RB * CB), jnp.int32),
            pltpu.SMEM((1, RB * CB), jnp.int32),
            dma((LOADS,)),
            dma,
            dma,
            dma((ITERS,)),
            dma((n,)),
            dma((n,)),
            dma((n,)),
            dma((n,)),
            dma((m * PIECES,)),
            dma(((m + 2) * PIECES,)),
            dma((m,)),
            dma((m + 2,)),
            dma((2 * m * PIECES,)),
            dma((m * PIECES,)),
            dma((2 * m,)),
            dma((m,)),
            dma((m,)),
            dma((m,)),
            dma((n,)),
            dma((2, n)),
        ],
        compiler_params=pltpu.CompilerParams(
            collective_id=0, has_side_effects=True, vmem_limit_bytes=56 * 1024 * 1024
        ),
        name="subspace",
    )(
        live_counts,
        row_blocks.reshape(1, slots),
        col_blocks.reshape(1, slots),
        sens_tiles,
        start_basis,
    )


def solution(mesh):
    in_specs = (
        P("blk", "rows", None),
        P(None, "blk"),
        P("blk", "rows"),
        P("blk", "rows"),
        P("blk", "rows"),
    )
    out_specs = P(None, None, ("blk", "rows"))
    return jax.shard_map(
        functools.partial(local, mesh.shape["blk"], mesh.shape["rows"]),
        mesh=mesh,
        in_specs=in_specs,
        out_specs=out_specs,
        check_vma=False,
    )
```
